512 devices in a mesh: gx: 16 (over y_hi, x, core), gy: 32 (over z, y_lo).
Axes of the slice: x: 4, y: 4 (y_hi: 2, y_lo: 2; y = y_hi * 2 + y_lo), z: 16, core: 2. Of those that a mesh axis runs over, the one named last changes fastest.
Arguments:
- velocity: float32 [2, 1, 2048, 2048], P(None, None, 'gy', 'gx'), may hold values from -6 to 6
- weights_x: float32 [4, 4096], replicated, may hold values from -0.25 to 0.75
- weights_y: float32 [4, 4096], replicated, may hold values from -0.25 to 0.75
- acoustic: bfloat16 [4, 1, 4096, 4096], P(None, None, 'gy', 'gx'), may hold values from -6 to 6
- wall_mask: int32 [1, 4096, 4096], P(None, 'gy', 'gx'), may hold values 0 or 1
Outputs:
- advanced: bfloat16 [4, 1, 4096, 4096], P(None, None, 'gy', 'gx')
The draws below stay inside these ranges and needn't reach their ends.
All inputs are finite; a program needn't handle non-finite values. No bound on the sum of `wall_mask` on one device may be relied on, other than what follows from the above.
Results may differ from the reference program's by a relative error of at most 0.002.
Values sent between devices are 32-bit elements; how exact they have to be, the bound alone decides.
A program may use at most 64 MiB of HBM per device.

```python
import jax
import jax.numpy as jnp

NX = 2048
NY = 2048
PLANES = 1
AX = 4096
AY = 4096


def touch_ends(values, own_key, smallest, top_value):
    longest = values.shape.index(max(values.shape))
    spots = []
    for shift in (0, 1):
        where = [jax.random.randint(jax.random.fold_in(own_key, axis), (), 0, length) for axis, length in enumerate(values.shape)]
        where[longest] = (where[longest] + shift) % values.shape[longest]
        spots.append(tuple(where))
    return values.at[spots[0]].set(smallest).at[spots[1]].set(top_value)


def block_levels(key, dims, cuts, low, top_value):
    gain = 1.0
    for dim, parts in cuts:
        steps = jax.random.uniform(jax.random.fold_in(jax.random.fold_in(key, 6), dim), (parts,), jnp.float32, low / len(cuts), top_value / len(cuts))
        gain = gain * jnp.repeat(jnp.exp(steps), dims[dim] // parts).reshape((-1,) + (1,) * (len(dims) - 1 - dim))
    return gain


def noise(key, dims, scale, reach, pieces=(), kind=jnp.bfloat16):
    values = scale * jax.random.normal(key, dims, jnp.float32)
    if pieces:
        values = values * block_levels(key, dims, pieces, -0.22, 0.18)
    return jnp.clip(values, -reach, reach).astype(kind)


def setup_inputs(seed: int = 0) -> dict:
    key_of = jax.random.split(jax.random.key(seed), 6)
    return {
        "velocity": noise(key_of[0], (2, PLANES, NY, NX), 1.0, 6.0, ((2, 32), (3, 16)), jnp.float32),
        "weights_x": jnp.clip(jax.random.uniform(key_of[1], (4, AX), jnp.float32, -0.25, 0.75), -0.25, 0.75),
        "weights_y": jnp.clip(jax.random.uniform(key_of[2], (4, AY), jnp.float32, -0.25, 0.75), -0.25, 0.75),
        "acoustic": noise(key_of[3], (4, PLANES, AY, AX), 1.0, 6.0, ((2, 32), (3, 16))),
        "wall_mask": touch_ends((jax.random.randint(key_of[4], (PLANES, AY, AX), 0, 8) < 1).astype(jnp.int32), jax.random.fold_in(key_of[4], 1), 0, 1),
    }


stencil_weights = (0.75, -0.15, 1.0 / 60.0)
mean_flow = 0.3
time_step = 0.5


def signed_wave(length):
    counts = jnp.arange(length)
    return jnp.where(counts < length // 2, counts, counts - length)


def refine_last(samples, weights):
    coarse = samples.shape[-1]
    fine_index = jnp.arange(2 * coarse) // 2
    result = jnp.zeros(samples.shape[:-1] + (2 * coarse,), samples.dtype)
    for offset in range(4):
        tapped = jnp.take(samples, (fine_index - 1 + offset) % coarse, axis=-1)
        result = result + tapped * weights[offset]
    return result


def gradients(padded):
    height = padded.shape[-2] - 6
    breadth = padded.shape[-1] - 6
    rows_mid = padded[..., 3:3 + height, :]
    cols_mid = padded[..., :, 3:3 + breadth]
    along_x = jnp.zeros_like(padded[..., 3:3 + height, 3:3 + breadth])
    along_y = jnp.zeros_like(along_x)
    for index, weight in enumerate(stencil_weights):
        distance = index + 1
        along_x = along_x + weight * (rows_mid[..., 3 + distance:3 + distance + breadth] - rows_mid[..., 3 - distance:3 - distance + breadth])
        along_y = along_y + weight * (cols_mid[..., 3 + distance:3 + distance + height, :] - cols_mid[..., 3 - distance:3 - distance + height, :])
    return along_x, along_y


def tendency(padded, source):
    along_x, along_y = gradients(padded)
    diverge = along_x[1] + along_y[2]
    forcing = jnp.stack([-diverge, -along_x[3], -along_y[3], source - diverge])
    return forcing - mean_flow * along_x


def reference(velocity, weights_x, weights_y, acoustic, wall_mask):
    real_type = velocity.dtype
    acoustic = acoustic.astype(real_type)
    flow_x = velocity[0]
    flow_y = velocity[1]
    tensor = jnp.stack([flow_x * flow_x, flow_x * flow_y, flow_y * flow_y])
    spectra = jnp.fft.fft2(tensor, axes=(-2, -1))
    wave_x = signed_wave(NX).astype(real_type)[None, :]
    wave_y = signed_wave(NY).astype(real_type)[:, None]
    numerator = -(wave_x * wave_x * spectra[0] + 2.0 * wave_x * wave_y * spectra[1] + wave_y * wave_y * spectra[2])
    denominator = wave_x * wave_x + wave_y * wave_y
    positive = denominator > 0
    solved = jnp.where(positive, numerator / jnp.where(positive, denominator, 1.0), 0.0)
    pressure = jnp.real(jnp.fft.ifft2(solved, axes=(-2, -1))).astype(real_type)
    source = refine_last(pressure, weights_x)
    source = jnp.swapaxes(refine_last(jnp.swapaxes(source, -1, -2), weights_y), -1, -2)
    open_cells = (1 - wall_mask).astype(real_type)
    widths = ((0, 0), (0, 0), (3, 3), (3, 3))
    first_rate = tendency(jnp.pad(acoustic, widths), source)
    middle = open_cells * (acoustic + time_step * first_rate)
    second_rate = tendency(jnp.pad(middle, widths), source)
    return (open_cells * (acoustic + 0.5 * time_step * (first_rate + second_rate))).astype(jnp.bfloat16)
```

```python
import functools
import math

import jax
import jax.numpy as jnp
import numpy as np
from jax import lax
from jax.experimental import pallas as pl
from jax.experimental.pallas import tpu as pltpu
from jax.sharding import PartitionSpec as P

F32 = jnp.float32
BF16 = jnp.bfloat16
MESH = pl.DeviceIdType.MESH
PX = 72


def two_parts(array):
    high = array.astype(BF16)
    low = (array - high.astype(np.float64)).astype(BF16)
    return np.stack([high, low])


def turn(products, modulus):
    return 2.0 * np.pi / modulus * np.mod(products, modulus).astype(np.float64)


@functools.lru_cache(maxsize=None)
def tables(ngx, ngy):
    nx, ny, ns, half = 128 * ngx, 64 * ngy, 64 // ngy, ngy // 2 + 1
    lane = np.arange(128)
    wide = np.arange(256) - 4
    place = (128 * np.arange(ngx)[:, None] + lane)[None] * np.arange(ngx)[:, None, None]
    angle = turn(place, nx)
    fx = np.concatenate([np.cos(angle), np.sin(angle)], axis=1).astype(np.float32)
    angle = turn(np.arange(64)[:, None] * lane[None], 128)
    plain = np.concatenate([np.cos(angle), np.sin(angle)], axis=1)
    first = plain.copy()
    first[0, 128:] = -((-1.0) ** lane)
    wx = np.stack([two_parts(plain), two_parts(first)])
    angle = turn(np.arange(half)[:, None] * (lane % 64)[None], ny)
    twf = np.stack([np.cos(angle), np.sin(angle)]).astype(np.float32)
    angle = turn(np.arange(64)[:, None] * np.arange(64)[None], 64)
    cos2 = np.kron(np.eye(2), np.cos(angle))
    sin2 = np.kron(np.eye(2), np.sin(angle))
    yf = two_parts(np.block([[cos2, -sin2], [sin2, cos2]]))
    angle = turn(np.arange(64)[:, None] * (lane - 4)[None], 64)
    cos2 = np.concatenate([np.cos(angle)] * 2)
    sin2 = np.concatenate([np.sin(angle)] * 2)
    yi = two_parts(np.block([[cos2, sin2], [-sin2, cos2]]))
    angle = turn(np.arange(half)[:, None] * (lane - 4)[None], ny)
    scale = np.full((half, 1), 2.0)
    scale[0] = scale[-1] = 1.0
    scale = scale / (nx * ny)
    twi = np.stack([scale * np.cos(angle), scale * np.sin(angle)]).astype(np.float32)
    k2 = np.arange(ngy)[:, None] + ngy * np.arange(ns)[None]
    angle = turn(k2[..., None] * wide, 128)
    cosine, sine = 2.0 * np.cos(angle), 2.0 * np.sin(angle)
    rows = np.zeros((ngy, 2, ns, 512))
    rows[:, 0, :, :256], rows[:, 0, :, 256:] = cosine, sine
    rows[:, 1, :, :256], rows[:, 1, :, 256:] = -sine, cosine
    packed = rows.copy()
    packed[0, 0, 0, :256], packed[0, 0, 0, 256:] = 1.0, 0.0
    packed[0, 1, 0, :256], packed[0, 1, 0, 256:] = (-1.0) ** wide, 0.0
    dx = np.stack([two_parts(rows.reshape(128, 512)), two_parts(packed.reshape(128, 512))])
    place = (128 * np.arange(ngx)[:, None] + wide)[:, None, :] * np.arange(ngx)[None, :, None]
    angle = turn(place, nx)
    cx = np.concatenate([np.cos(angle), np.sin(angle)], axis=1).astype(np.float32)
    return fx, wx, twf, yf, twi, yi, dx, cx


def rfft(values):
    count = len(values)
    if count == 1:
        return [(values[0], None)]
    even, odd = rfft(values[0::2]), rfft(values[1::2])
    if count == 2:
        return [(even[0][0] + odd[0][0], None), (even[0][0] - odd[0][0], None)]
    middle = count // 2

    def full(half, k):
        k = k % middle
        if k <= middle // 2:
            return half[k]
        real, imag = half[middle - k]
        return (real, None if imag is None else -imag)

    result = []
    for k in range(middle + 1):
        er, ei = full(even, k)
        orr, oi = full(odd, k)
        if k == 0:
            result.append((er + orr, None))
        elif k == middle:
            result.append((er - orr, None))
        elif 2 * k == middle:
            result.append((er, -orr))
        else:
            c, s = math.cos(2 * math.pi * k / count), math.sin(2 * math.pi * k / count)
            tr = c * orr + (0.0 if oi is None else s * oi)
            ti = (0.0 if oi is None else c * oi) - s * orr
            result.append((er + tr, ti if ei is None else ei + ti))
    return result


def real_sum(spectrum):
    middle = len(spectrum) - 1
    if middle == 1:
        a, b = spectrum[0][0], spectrum[1][0]
        return [a + b, a - b]
    count = 2 * middle

    def fold(values):
        folded = []
        for k in range(middle // 2 + 1):
            if 2 * k == middle:
                folded.append((values[k][0], None))
                continue
            ar, ai = values[k]
            br, bi = values[middle - k]
            if k == 0:
                folded.append((ar + br, None))
            else:
                folded.append((ar + br, ai - bi))
        return folded

    twisted = []
    for k in range(middle + 1):
        vr, vi = spectrum[k]
        if k == 0:
            twisted.append((vr, None))
        elif k == middle:
            twisted.append((-vr, None))
        elif 2 * k == middle:
            twisted.append((-vi, vr))
        else:
            c, s = math.cos(2 * math.pi * k / count), math.sin(2 * math.pi * k / count)
            twisted.append((c * vr - s * vi, c * vi + s * vr))
    even, odd = real_sum(fold(spectrum)), real_sum(fold(twisted))
    result = []
    for a, b in zip(even, odd):
        result += [a, b]
    return result


def parts(value):
    high = value.astype(BF16)
    return high, (value - high.astype(F32)).astype(BF16)


def dot(a, b):
    return jnp.dot(a, b, preferred_element_type=F32)


def dot3(left, right):
    lh, ll = left
    rh, rl = right
    return dot(lh, rh) + dot(lh, rl) + dot(ll, rh)


def dot_t(a, b):
    return lax.dot_general(a, b, (((1,), (1,)), ((), ())), preferred_element_type=F32)


def shifted(value, step):
    width = value.shape[-1]
    return pltpu.roll(value, (-step) % width, value.ndim - 1)


WEIGHTS = (0.75, -0.15, 1.0 / 60.0)


def slope_x(value):
    total = None
    for index, weight in enumerate(WEIGHTS):
        term = weight * (shifted(value, index + 1) - shifted(value, -index - 1))
        total = term if total is None else total + term
    return total


def slope_y(window, rows):
    total = None
    for index, weight in enumerate(WEIGHTS):
        k = index + 1
        term = weight * (window[8 + k : 8 + k + rows] - window[8 - k : 8 - k + rows])
        total = term if total is None else total + term
    return total


def kernel(
    ngx, ngy,
    vel, weights_x, weights_y, ac, wall, fx, wx, twf, yf, twi, yi, dx, cx,
    out,
    vg, acs, wls, wxs, wys, fxs, wxm, twfs, yfs, twis, yis, dxs, cxs,
    ext, mid, adv, pack, xsend, xrecv, ax, ay, k1, k2,
    zs, b3, r3, gs, ps, us, b4, r4, s4, sb, sg, qs,
    loc, x_send, x_recv, y_send, y_recv, h_send, h_recv, v_send, v_recv, w_send, w_recv,
):
    ns, half = 64 // ngy, ngy // 2 + 1
    rpm = max(8, 3 * ns)
    i, j = lax.axis_index("gx"), lax.axis_index("gy")
    partner = i + 1 - 2 * (i % 2)
    right, left = (i + 1) % ngx, (i + ngx - 1) % ngx
    down, up = (j + 1) % ngy, (j + ngy - 1) % ngy
    chips = ngx // 2

    barrier = pltpu.get_barrier_semaphore()

    def greet_y(k, carry):
        pl.semaphore_signal(barrier, inc=1, device_id={"gy": (j + k) % ngy}, device_id_type=MESH)
        return carry

    def greet_x(k, carry):
        pl.semaphore_signal(barrier, inc=1, device_id={"gx": (i + 2 * k) % ngx}, device_id_type=MESH)
        return carry

    lax.fori_loop(1, ngy, greet_y, 0)
    lax.fori_loop(1, chips, greet_x, 0)
    pl.semaphore_signal(barrier, inc=1, device_id={"gx": right}, device_id_type=MESH)
    pl.semaphore_signal(barrier, inc=1, device_id={"gx": left}, device_id_type=MESH)

    first = jnp.where(i == 0, 1, 0)
    sources = [
        (ac, acs), (wall, wls), (weights_x, wxs), (weights_y, wys), (vel, vg.at[i]),
        (fx.at[i], fxs), (wx.at[first], wxm), (twf, twfs), (yf, yfs), (twi, twis), (yi, yis),
        (dx, dxs), (cx.at[i], cxs),
    ]
    copies = [pltpu.make_async_copy(a, b, loc.at[n]) for n, (a, b) in enumerate(sources)]
    for copy in copies:
        copy.start()

    row = lax.broadcasted_iota(jnp.int32, (rpm, 128), 0)
    lane = lax.broadcasted_iota(jnp.int32, (rpm, 128), 1)
    field, slot = row // ns, row % ns
    wave = i + ngx * (j + ngy * slot)
    is_packed = wave == 0
    in_imag = lane >= 64
    wave_x = jnp.where(is_packed & in_imag, 64 * ngx, wave).astype(F32)

    def coefficients(q, carry):
        index = q + ngy * (lane % 64)
        wave_y = jnp.where(index >= 32 * ngy, index - 64 * ngy, index).astype(F32)
        xx, yy = wave_x * wave_x, wave_y * wave_y
        inverse = -1.0 / jnp.maximum(xx + yy, 1.0)
        k1[q] = jnp.where(field == 0, xx * inverse, jnp.where(field == 2, yy * inverse, 0.0))
        cross = (field == 1) & jnp.logical_not(is_packed) & (index != 32 * ngy)
        k2[q] = jnp.where(cross, 2.0 * wave_x * wave_y * inverse, 0.0)
        return carry

    lax.fori_loop(0, half, coefficients, 0)

    ext[:, 0:8, :] = jnp.zeros((5, 8, 384), F32)
    ext[:, 152:160, :] = jnp.zeros((5, 8, 384), F32)
    b3[...] = jnp.zeros(b3.shape, F32)
    copies[0].wait()
    copies[1].wait()
    for v in range(4):
        ext[v, 16:144, 0:256] = acs[v].astype(F32)
    ext[4, 16:144, 0:256] = 1.0 - wls[...].astype(F32)

    copies[2].wait()
    copies[3].wait()

    def tile_of(ref, column):
        return ref[:, pl.ds(pl.multiple_of(column, 128), 128)]

    narrow = lax.broadcasted_iota(jnp.int32, (4, 128), 1)
    total_x, total_y = 256 * ngx, 128 * ngy
    outer = jnp.where(
        narrow < 64,
        tile_of(wxs, (256 * i + 256) % total_x),
        tile_of(wxs, (256 * i + total_x - 128) % total_x),
    )
    tiles = [tile_of(wxs, 256 * i), tile_of(wxs, 256 * i + 128), outer]
    for t, weights in enumerate(tiles):
        fine = 128 * t + lax.broadcasted_iota(jnp.int32, (256, 128), 1)
        fine = jnp.where(fine < 320, fine, fine - 384) + 16
        coarse = lax.broadcasted_iota(jnp.int32, (256, 128), 0) - 4
        tap = coarse - (fine // 2 - 8 - 1)
        matrix = jnp.zeros((256, 128), F32)
        for s in range(4):
            matrix = matrix + jnp.where(tap == s, weights[s : s + 1, :], 0.0)
        high, low = parts(matrix)
        ax[0, :, 128 * t : 128 * t + 128] = high
        ax[1, :, 128 * t : 128 * t + 128] = low
    outer = jnp.where(
        narrow < 64,
        tile_of(wys, (128 * j + 128) % total_y),
        tile_of(wys, (128 * j + total_y - 128) % total_y),
    )
    for t, weights in enumerate([tile_of(wys, 128 * j), outer]):
        fine = 128 * t + lax.broadcasted_iota(jnp.int32, (128, 128), 1)
        fine = jnp.where(fine < 192, fine, fine - 256) + 16
        coarse = lax.broadcasted_iota(jnp.int32, (128, 128), 0) - 4
        tap = coarse - (fine // 2 - 8 - 1)
        matrix = jnp.zeros((128, 128), F32)
        for s in range(4):
            matrix = matrix + jnp.where(tap == s, weights[s : s + 1, :], 0.0)
        high, low = parts(jnp.transpose(matrix))
        ay[0, 128 * t : 128 * t + 128, :] = high
        ay[1, 128 * t : 128 * t + 128, :] = low

    pl.semaphore_wait(barrier, ngy - 1 + chips - 1 + 2)

    def gather(source, own, slots, send, recv):
        def direct(k):
            return pltpu.make_async_remote_copy(
                src_ref=source, dst_ref=slots.at[own], send_sem=send.at[k], recv_sem=recv.at[own],
                device_id={"gx": (own + 2 * k) % ngx}, device_id_type=MESH,
            )

        def to_partner(block, at, k):
            return pltpu.make_async_remote_copy(
                src_ref=block, dst_ref=slots.at[at], send_sem=send.at[k], recv_sem=recv.at[at],
                device_id={"gx": partner}, device_id_type=MESH,
            )

        def arrived(at):
            pltpu.make_async_remote_copy(
                src_ref=slots.at[at], dst_ref=slots.at[at], send_sem=send.at[0], recv_sem=recv.at[at],
                device_id={"gx": partner}, device_id_type=MESH,
            ).wait_recv()

        def start():
            def go(k, carry):
                direct(k).start()
                return carry

            lax.fori_loop(1, chips, go, 0)
            to_partner(source, own, 0).start()

        def relay():
            def step(k, carry):
                at = (own + ngx - 2 * k) % ngx
                arrived(at)
                to_partner(slots.at[at], at, chips - 1 + k).start()
                return carry

            lax.fori_loop(1, chips, step, 0)

            def rest(k, carry):
                arrived((partner + ngx - 2 * k) % ngx)
                return carry

            lax.fori_loop(0, chips, rest, 0)

        def finish():
            def step(k, carry):
                direct(k).wait_send()
                to_partner(slots.at[own], own, chips - 1 + k).wait_send()
                return carry

            lax.fori_loop(1, chips, step, 0)
            to_partner(source, own, 0).wait_send()

        return start, relay, finish

    start1, relay1, finish1 = gather(vel, i, vg, x_send, x_recv)
    start1()

    def strip(to, rows_from, rows_to, n):
        return pltpu.make_async_remote_copy(
            src_ref=ext.at[:, pl.ds(rows_from, 8), pl.ds(0, 256)],
            dst_ref=ext.at[:, pl.ds(rows_to, 8), pl.ds(0, 256)],
            send_sem=h_send.at[n], recv_sem=h_recv.at[n],
            device_id={"gy": to}, device_id_type=MESH,
        )

    go_down, go_up = strip(down, 136, 8, 0), strip(up, 16, 144, 1)
    go_down.start()
    go_up.start()
    go_down.wait()
    go_up.wait()
    ext[:, 8:16, 0:256] = jnp.where(j > 0, ext[:, 8:16, 0:256], 0.0)
    ext[:, 144:152, 0:256] = jnp.where(j < ngy - 1, ext[:, 144:152, 0:256], 0.0)

    strip_lane = lax.broadcasted_iota(jnp.int32, (144, 128), 1)
    for side in range(2):
        packed = jnp.zeros((144, 128), F32)
        for v in range(5):
            if side == 0:
                moved = pltpu.roll(ext[v, 8:152, 128:256], (8 * v - 120) % 128, 1)
            else:
                moved = pltpu.roll(ext[v, 8:152, 0:128], 8 * v, 1) if v else ext[v, 8:152, 0:128]
            packed = jnp.where((strip_lane >= 8 * v) & (strip_lane < 8 * v + 8), moved, packed)
        xsend[side] = packed

    relay1()

    def column(to, n):
        return pltpu.make_async_remote_copy(
            src_ref=xsend.at[n], dst_ref=xrecv.at[n],
            send_sem=h_send.at[2 + n], recv_sem=h_recv.at[2 + n],
            device_id={"gx": to}, device_id_type=MESH,
        )

    go_right, go_left = column(right, 0), column(left, 1)
    go_right.start()
    go_left.start()

    for n in (4, 5, 6):
        copies[n].wait()

    def combine(c, carry):
        rows = pl.ds(pl.multiple_of(8 * c, 8), 8)
        sums = [None] * 6
        for d in range(ngx):
            u, v = vg[d, 0, rows, :], vg[d, 1, rows, :]
            cosine, sine = fxs[d : d + 1, :], fxs[ngx + d : ngx + d + 1, :]
            for f, value in enumerate((u * u, u * v, v * v)):
                real, imag = value * cosine, value * sine
                sums[2 * f] = real if d == 0 else sums[2 * f] + real
                sums[2 * f + 1] = -imag if d == 0 else sums[2 * f + 1] - imag
        for f in range(3):
            zs[f, 0, rows, :] = sums[2 * f]
            zs[f, 1, rows, :] = sums[2 * f + 1]
        return carry

    lax.fori_loop(0, 8, combine, 0)
    w_high, w_low = wxm[0], wxm[1]
    for f in range(3):
        pieces = []
        for real, imag in zip(parts(zs[f, 0]), parts(zs[f, 1])):
            plain = jnp.concatenate([real, imag], axis=1)
            turned = jnp.concatenate([imag, -real], axis=1)
            both = [turned, -plain] if f == 1 else [plain, turned]
            pieces.append(jnp.concatenate(both, axis=0))
        high, low = pieces
        lines = dot_t(w_high, high) + dot_t(w_high, low) + dot_t(w_low, high)
        for s in range(ns):
            b3[pl.ds(ns * f + s, ngy, stride=rpm), :] = lines[ngy * s : ngy * s + ngy]

    def offset(m):
        step = (m + 1) // 2
        return ngy // 2 + jnp.where(m % 2 == 1, step, -step)

    def send3(k):
        to = (j + k) % ngy
        return pltpu.make_async_remote_copy(
            src_ref=b3.at[pl.ds(pl.multiple_of(to * rpm, 8), rpm), :], dst_ref=r3.at[j],
            send_sem=y_send.at[k], recv_sem=y_recv.at[j],
            device_id={"gy": to}, device_id_type=MESH,
        )

    def recv3(d):
        return pltpu.make_async_remote_copy(
            src_ref=r3.at[d], dst_ref=r3.at[d], send_sem=y_send.at[0], recv_sem=y_recv.at[d],
            device_id={"gy": d}, device_id_type=MESH,
        )

    def go3(m, carry):
        send3(offset(m)).start()
        return carry

    lax.fori_loop(0, ngy - 1, go3, 0)
    r3[j] = b3[pl.ds(pl.multiple_of(j * rpm, 8), rpm), :]

    go_right.wait()
    go_left.wait()
    for v in range(5):
        from_right = pltpu.roll(xrecv[1], (-8 * v) % 128, 1) if v else xrecv[1]
        from_left = pltpu.roll(xrecv[0], 120 - 8 * v, 1)
        from_right = jnp.where((strip_lane < 8) & (i < ngx - 1), from_right, 0.0)
        ext[v, 8:152, 256:384] = jnp.where((strip_lane >= 120) & (i > 0), from_left, from_right)

    def rates(planes, at, rows):
        here = pl.ds(at, rows)
        window = pl.ds(pl.multiple_of(at - 8, 8), rows + 16)
        b_window, p_window = planes[2, window, :], planes[3, window, :]
        b, p = b_window[8 : 8 + rows], p_window[8 : 8 + rows]
        rho, a = planes[0, here, :], planes[1, here, :]
        slope_b, slope_p = slope_y(b_window, rows), slope_y(p_window, rows)
        return (
            (rho, slope_x(a + 0.3 * rho) + slope_b),
            (a, slope_x(p + 0.3 * a)),
            (b, slope_x(0.3 * b) + slope_p),
            (p, slope_x(a + 0.3 * p) + slope_b),
        )

    def stage_one(c, carry):
        at = pl.multiple_of(8 + 8 * c, 8)
        here = pl.ds(at, 8)
        open_cells = ext[4, here, :]
        for v, (value, rate) in enumerate(rates(ext, at, 8)):
            mid[v, here, :] = open_cells * (value - 0.5 * rate)
            adv[v, here, :] = (value - 0.25 * rate)[:, 0:256]
        return carry

    lax.fori_loop(0, 18, stage_one, 0)

    def stage_two(c, carry):
        at = pl.multiple_of(16 + 8 * c, 8)
        here = pl.ds(at, 8)
        open_cells = ext[4, here, 0:256]
        for v, (value, rate) in enumerate(rates(mid, at, 8)):
            adv[v, here, :] = open_cells * (adv[v, here, :] - 0.25 * rate[:, 0:256])
        return carry

    lax.fori_loop(0, 16, stage_two, 0)

    def got3(k, carry):
        recv3((j + k) % ngy).wait_recv()
        return carry

    for n in range(7, 13):
        copies[n].wait()
    lax.fori_loop(1, ngy, got3, 0)

    spectrum = rfft([r3[d] for d in range(ngy)])
    for q, (real, imag) in enumerate(spectrum):
        rows = slice(rpm * q, rpm * q + rpm)
        cosine, sine = twfs[0, q : q + 1, :], twfs[1, q : q + 1, :]
        if imag is None:
            gs[rows, 0:128] = real * cosine
            gs[rows, 128:256] = -(real * sine)
        else:
            gs[rows, 0:128] = real * cosine + imag * sine
            gs[rows, 128:256] = imag * cosine - real * sine
    gs[...] = dot3(parts(gs[...]), (yfs[0], yfs[1]))
    corner = (row == ns) & (lane == 96) & (i == 0) & (j == 0)
    row_lane = lax.broadcasted_iota(jnp.int32, (ns, 128), 1)
    for q in range(half):
        real, imag = gs[rpm * q : rpm * q + rpm, 0:128], gs[rpm * q : rpm * q + rpm, 128:256]
        total_real = k1[q] * real - k2[q] * imag
        total_imag = k1[q] * imag + k2[q] * real
        if q == 0:
            total_real = total_real - jnp.where(corner, pltpu.roll(real, 64, 1), 0.0)
            total_imag = total_imag - jnp.where(corner, pltpu.roll(imag, 64, 1), 0.0)
        for n, total in enumerate((total_real, total_imag)):
            value = total[0:ns] + total[ns : 2 * ns] + total[2 * ns : 3 * ns]
            lanes = slice(128 * n, 128 * n + 128)
            at = 2 * ns * q
            ps[at : at + ns, lanes] = jnp.where(row_lane < 64, value, 0.0)
            ps[at + ns : at + 2 * ns, lanes] = jnp.where(row_lane < 64, 0.0, value)
    us[...] = dot3(parts(ps[...]), (yis[0], yis[1]))
    terms = []
    for q in range(half):
        rows = slice(2 * ns * q, 2 * ns * q + 2 * ns)
        real, imag = us[rows, 0:128], us[rows, 128:256]
        cosine, sine = twis[0, q : q + 1, :], twis[1, q : q + 1, :]
        turned_real = real * cosine - imag * sine
        if q in (0, half - 1):
            terms.append((turned_real, None))
        else:
            terms.append((turned_real, real * sine + imag * cosine))
    for d, value in enumerate(real_sum(terms)):
        b4[d] = value

    def send4(k):
        to = (j + k) % ngy
        return pltpu.make_async_remote_copy(
            src_ref=b4.at[to], dst_ref=r4.at[j], send_sem=v_send.at[k], recv_sem=v_recv.at[j],
            device_id={"gy": to}, device_id_type=MESH,
        )

    def recv4(d):
        return pltpu.make_async_remote_copy(
            src_ref=r4.at[d], dst_ref=r4.at[d], send_sem=v_send.at[0], recv_sem=v_recv.at[d],
            device_id={"gy": d}, device_id_type=MESH,
        )

    def go4(m, carry):
        send4(offset(m)).start()
        return carry

    def got4(k, carry):
        recv4((j + k) % ngy).wait_recv()
        return carry

    lax.fori_loop(0, ngy - 1, go4, 0)
    r4[j] = b4[j]
    lax.fori_loop(1, ngy, got4, 0)
    for g in range(ngy):
        s4[2 * ns * g : 2 * ns * g + 2 * ns, :] = r4[g]
    sb[...] = jnp.transpose(s4[...])[0:PX]
    start2, relay2, finish2 = gather(sb, i, sg, w_send, w_recv)
    start2()
    sg[i] = sb[...]
    relay2()

    pressure = jnp.zeros((PX, 256), F32)
    blocks = [(0, 1, 1)] + [(a, min(a + 5, ngx), 0) for a in range(1, ngx, 5)]
    for begin, end, variant in blocks:
        lines = sg[begin:end].reshape((end - begin) * PX, 128)
        mixed = dot3(parts(lines), (dxs[variant, 0], dxs[variant, 1]))
        for n in range(begin, end):
            rows = slice((n - begin) * PX, (n - begin + 1) * PX)
            cosine, sine = cxs[n : n + 1, :], cxs[ngx + n : ngx + n + 1, :]
            pressure = pressure + (mixed[rows, 0:256] * cosine - mixed[rows, 256:512] * sine)

    along = dot3(parts(pressure), (ax[0], ax[1]))
    along = jnp.concatenate([along, jnp.zeros((128 - PX, 384), F32)], axis=0)
    source = dot3((ay[0], ay[1]), parts(along))
    qs[16:152, :] = 0.5 * ext[4, 16:152, :] * source[0:136]
    qs[8:16, :] = 0.5 * ext[4, 8:16, :] * source[248:256]
    qs[0:8, :] = jnp.zeros((8, 384), F32)
    qs[152:160, :] = jnp.zeros((8, 384), F32)

    def last(c, carry):
        at = pl.multiple_of(16 + 16 * c, 16)
        here = pl.ds(at, 16)
        there = pl.ds(pl.multiple_of(16 * c, 16), 16)
        window = qs[pl.ds(pl.multiple_of(at - 8, 8), 32), :]
        half_source = window[8:24]
        quarter = 0.25 * ext[4, here, 0:256]
        change_x = quarter * slope_x(half_source)[:, 0:256]
        change_y = quarter * slope_y(window, 16)[:, 0:256]
        out[0, there, :] = adv[0, here, :].astype(BF16)
        out[1, there, :] = (adv[1, here, :] - change_x).astype(BF16)
        out[2, there, :] = (adv[2, here, :] - change_y).astype(BF16)
        out[3, there, :] = (adv[3, here, :] + half_source[:, 0:256] - 0.3 * change_x).astype(BF16)
        return carry

    lax.fori_loop(0, 8, last, 0)

    finish1()
    finish2()

    def left3(k, carry):
        send3(k).wait_send()
        return carry

    def left4(k, carry):
        send4(k).wait_send()
        return carry

    lax.fori_loop(1, ngy, left3, 0)
    lax.fori_loop(1, ngy, left4, 0)


def solution(mesh):
    ngx, ngy = mesh.shape["gx"], mesh.shape["gy"]
    ns, half = 64 // ngy, ngy // 2 + 1
    rpm = max(8, 3 * ns)
    consts = tables(ngx, ngy)

    def shards(velocity, weights_x, weights_y, acoustic, wall_mask):
        vel = velocity.reshape(2, 64, 128)
        ac = acoustic.reshape(4, 128, 256)
        wall = wall_mask.reshape(128, 256)
        fx, wx, twf, yf, twi, yi, dx, cx = [jnp.asarray(c) for c in consts]
        anywhere = pl.BlockSpec(memory_space=pl.ANY)
        vmem = pltpu.VMEM
        dma = pltpu.SemaphoreType.DMA
        scratch = [
            vmem((ngx, 2, 64, 128), F32),
            vmem((4, 128, 256), BF16),
            vmem((128, 256), jnp.int32),
            vmem((4, 256 * ngx), F32),
            vmem((4, 128 * ngy), F32),
            vmem(fx.shape[1:], F32),
            vmem(wx.shape[1:], BF16),
            vmem(twf.shape, F32),
            vmem(yf.shape, BF16),
            vmem(twi.shape, F32),
            vmem(yi.shape, BF16),
            vmem(dx.shape, BF16),
            vmem(cx.shape[1:], F32),
            vmem((5, 160, 384), F32),
            vmem((4, 160, 384), F32),
            vmem((4, 160, 256), F32),
            vmem((8, 128), F32),
            vmem((2, 144, 128), F32),
            vmem((2, 144, 128), F32),
            vmem((2, 256, 384), BF16),
            vmem((2, 256, 128), BF16),
            vmem((half, rpm, 128), F32),
            vmem((half, rpm, 128), F32),
            vmem((3, 2, 64, 128), F32),
            vmem((ngy * rpm, 128), F32),
            vmem((ngy, rpm, 128), F32),
            vmem((half * rpm, 256), F32),
            vmem((half * 2 * ns, 256), F32),
            vmem((half * 2 * ns, 256), F32),
            vmem((ngy, 2 * ns, 128), F32),
            vmem((ngy, 2 * ns, 128), F32),
            vmem((128, 128), F32),
            vmem((PX, 128), F32),
            vmem((ngx, PX, 128), F32),
            vmem((160, 384), F32),
            dma((13,)),
            dma((ngx,)), dma((ngx,)),
            dma((ngy,)), dma((ngy,)),
            dma((4,)), dma((4,)),
            dma((ngy,)), dma((ngy,)),
            dma((ngx,)), dma((ngx,)),
        ]
        result = pl.pallas_call(
            functools.partial(kernel, ngx, ngy),
            out_shape=jax.ShapeDtypeStruct((4, 128, 256), BF16),
            in_specs=[anywhere] * 13,
            out_specs=pl.BlockSpec(memory_space=pltpu.VMEM),
            scratch_shapes=scratch,
            compiler_params=pltpu.CompilerParams(
                collective_id=0, has_side_effects=True, vmem_limit_bytes=40 * 1024 * 1024
            ),
            name="poisson_step",
        )(vel, weights_x, weights_y, ac, wall, fx, wx, twf, yf, twi, yi, dx, cx)
        return result.reshape(4, 1, 128, 256)

    in_specs = (P(None, None, "gy", "gx"), P(), P(), P(None, None, "gy", "gx"), P(None, "gy", "gx"))
    return jax.shard_map(
        shards, mesh=mesh, in_specs=in_specs, out_specs=P(None, None, "gy", "gx"), check_vma=False
    )
```

```python
import functools
import math

import jax
import jax.numpy as jnp
import numpy as np
from jax import lax
from jax.experimental import pallas as pl
from jax.experimental.pallas import tpu as pltpu
from jax.sharding import PartitionSpec as P

F32 = jnp.float32
BF16 = jnp.bfloat16
MESH = pl.DeviceIdType.MESH
PX = 72


def two_parts(array):
    high = array.astype(BF16)
    low = (array - high.astype(np.float64)).astype(BF16)
    return np.stack([high, low])


def turn(products, modulus):
    return 2.0 * np.pi / modulus * np.mod(products, modulus).astype(np.float64)


@functools.lru_cache(maxsize=None)
def tables(ngx, ngy):
    nx, ny, ns, half = 128 * ngx, 64 * ngy, 64 // ngy, ngy // 2 + 1
    lane = np.arange(128)
    wide = np.arange(256) - 4
    place = (128 * np.arange(ngx)[:, None] + lane)[None] * np.arange(ngx)[:, None, None]
    angle = turn(place, nx)
    fx = np.concatenate([np.cos(angle), np.sin(angle)], axis=1).astype(np.float32)
    angle = turn(np.arange(64)[:, None] * lane[None], 128)
    plain = np.concatenate([np.cos(angle), np.sin(angle)], axis=1)
    first = plain.copy()
    first[0, 128:] = -((-1.0) ** lane)
    wx = np.stack([two_parts(plain), two_parts(first)])
    angle = turn(np.arange(half)[:, None] * (lane % 64)[None], ny)
    twf = np.stack([np.cos(angle), np.sin(angle)]).astype(np.float32)
    angle = turn(np.arange(64)[:, None] * np.arange(64)[None], 64)
    cos2 = np.kron(np.eye(2), np.cos(angle))
    sin2 = np.kron(np.eye(2), np.sin(angle))
    yf = two_parts(np.block([[cos2, -sin2], [sin2, cos2]]))
    angle = turn(np.arange(64)[:, None] * (lane - 4)[None], 64)
    cos2 = np.concatenate([np.cos(angle)] * 2)
    sin2 = np.concatenate([np.sin(angle)] * 2)
    yi = two_parts(np.block([[cos2, sin2], [-sin2, cos2]]))
    angle = turn(np.arange(half)[:, None] * (lane - 4)[None], ny)
    scale = np.full((half, 1), 2.0)
    scale[0] = scale[-1] = 1.0
    scale = scale / (nx * ny)
    twi = np.stack([scale * np.cos(angle), scale * np.sin(angle)]).astype(np.float32)
    k2 = np.arange(ngy)[:, None] + ngy * np.arange(ns)[None]
    angle = turn(k2[..., None] * wide, 128)
    cosine, sine = 2.0 * np.cos(angle), 2.0 * np.sin(angle)
    rows = np.zeros((ngy, 2, ns, 512))
    rows[:, 0, :, :256], rows[:, 0, :, 256:] = cosine, sine
    rows[:, 1, :, :256], rows[:, 1, :, 256:] = -sine, cosine
    packed = rows.copy()
    packed[0, 0, 0, :256], packed[0, 0, 0, 256:] = 1.0, 0.0
    packed[0, 1, 0, :256], packed[0, 1, 0, 256:] = (-1.0) ** wide, 0.0
    dx = np.stack([two_parts(rows.reshape(128, 512)), two_parts(packed.reshape(128, 512))])
    place = (128 * np.arange(ngx)[:, None] + wide)[:, None, :] * np.arange(ngx)[None, :, None]
    angle = turn(place, nx)
    cx = np.concatenate([np.cos(angle), np.sin(angle)], axis=1).astype(np.float32)
    return fx, wx, twf, yf, twi, yi, dx, cx


def rfft(values):
    count = len(values)
    if count == 1:
        return [(values[0], None)]
    even, odd = rfft(values[0::2]), rfft(values[1::2])
    if count == 2:
        return [(even[0][0] + odd[0][0], None), (even[0][0] - odd[0][0], None)]
    middle = count // 2

    def full(half, k):
        k = k % middle
        if k <= middle // 2:
            return half[k]
        real, imag = half[middle - k]
        return (real, None if imag is None else -imag)

    result = []
    for k in range(middle + 1):
        er, ei = full(even, k)
        orr, oi = full(odd, k)
        if k == 0:
            result.append((er + orr, None))
        elif k == middle:
            result.append((er - orr, None))
        elif 2 * k == middle:
            result.append((er, -orr))
        else:
            c, s = math.cos(2 * math.pi * k / count), math.sin(2 * math.pi * k / count)
            tr = c * orr + (0.0 if oi is None else s * oi)
            ti = (0.0 if oi is None else c * oi) - s * orr
            result.append((er + tr, ti if ei is None else ei + ti))
    return result


def real_sum(spectrum):
    middle = len(spectrum) - 1
    if middle == 1:
        a, b = spectrum[0][0], spectrum[1][0]
        return [a + b, a - b]
    count = 2 * middle

    def fold(values):
        folded = []
        for k in range(middle // 2 + 1):
            if 2 * k == middle:
                folded.append((values[k][0], None))
                continue
            ar, ai = values[k]
            br, bi = values[middle - k]
            if k == 0:
                folded.append((ar + br, None))
            else:
                folded.append((ar + br, ai - bi))
        return folded

    twisted = []
    for k in range(middle + 1):
        vr, vi = spectrum[k]
        if k == 0:
            twisted.append((vr, None))
        elif k == middle:
            twisted.append((-vr, None))
        elif 2 * k == middle:
            twisted.append((-vi, vr))
        else:
            c, s = math.cos(2 * math.pi * k / count), math.sin(2 * math.pi * k / count)
            twisted.append((c * vr - s * vi, c * vi + s * vr))
    even, odd = real_sum(fold(spectrum)), real_sum(fold(twisted))
    result = []
    for a, b in zip(even, odd):
        result += [a, b]
    return result


def parts(value):
    high = value.astype(BF16)
    return high, (value - high.astype(F32)).astype(BF16)


def dot(a, b):
    return jnp.dot(a, b, preferred_element_type=F32)


def dot3(left, right):
    lh, ll = left
    rh, rl = right
    return dot(lh, rh) + dot(lh, rl) + dot(ll, rh)


def dot_t(a, b):
    return lax.dot_general(a, b, (((1,), (1,)), ((), ())), preferred_element_type=F32)


def shifted(value, step):
    width = value.shape[-1]
    return pltpu.roll(value, (-step) % width, value.ndim - 1)


WEIGHTS = (0.75, -0.15, 1.0 / 60.0)


def slope_x(value):
    total = None
    for index, weight in enumerate(WEIGHTS):
        term = weight * (shifted(value, index + 1) - shifted(value, -index - 1))
        total = term if total is None else total + term
    return total


def slope_y(window, rows):
    total = None
    for index, weight in enumerate(WEIGHTS):
        k = index + 1
        term = weight * (window[8 + k : 8 + k + rows] - window[8 - k : 8 - k + rows])
        total = term if total is None else total + term
    return total


def kernel(
    ngx, ngy,
    vel, weights_x, weights_y, ac, wall, fx, wx, twf, yf, twi, yi, dx, cx,
    out,
    vg, acs, wls, wxs, wys, fxs, wxm, twfs, yfs, twis, yis, dxs, cxs,
    ext, mid, adv, xsend, xrecv, ax, ay, k1, k2,
    zs, b3, r3, gs, ps, us, b4, r4, s4, sb, sg, qs,
    loc, x_send, x_recv, y_send, y_recv, h_send, h_recv, v_send, v_recv, w_send, w_recv, token,
):
    ns, half = 64 // ngy, ngy // 2 + 1
    rpm = max(8, 3 * ns)
    i, j = lax.axis_index("gx"), lax.axis_index("gy")
    partner = i + 1 - 2 * (i % 2)
    right, left = (i + 1) % ngx, (i + ngx - 1) % ngx
    down, up = (j + 1) % ngy, (j + ngy - 1) % ngy
    chips = ngx // 2

    barrier = pltpu.get_barrier_semaphore()
    near = ngy // 4

    def greet_y(k, carry):
        pl.semaphore_signal(barrier, inc=1, device_id={"gy": (j + k) % ngy}, device_id_type=MESH)
        pl.semaphore_signal(
            barrier, inc=1, device_id={"gy": (j + ngy - k) % ngy}, device_id_type=MESH
        )
        return carry

    def greet_x(k, carry):
        pl.semaphore_signal(barrier, inc=1, device_id={"gx": (i + 2 * k) % ngx}, device_id_type=MESH)
        return carry

    lax.fori_loop(1, near + 1, greet_y, 0)
    lax.fori_loop(1, chips, greet_x, 0)
    pl.semaphore_signal(barrier, inc=1, device_id={"gx": right}, device_id_type=MESH)
    pl.semaphore_signal(barrier, inc=1, device_id={"gx": left}, device_id_type=MESH)

    first = jnp.where(i == 0, 1, 0)
    sources = [
        (ac, acs), (wall, wls), (weights_x, wxs), (weights_y, wys), (vel, vg.at[i]),
        (fx.at[i], fxs), (wx.at[first], wxm), (twf, twfs), (yf, yfs), (twi, twis), (yi, yis),
        (dx, dxs), (cx.at[i], cxs),
    ]
    copies = [pltpu.make_async_copy(a, b, loc.at[n]) for n, (a, b) in enumerate(sources)]
    for copy in copies:
        copy.start()

    pl.semaphore_wait(barrier, 2 * near + chips - 1 + 2)

    def gather(source, own, slots, send, recv):
        def direct(k):
            return pltpu.make_async_remote_copy(
                src_ref=source, dst_ref=slots.at[own], send_sem=send.at[k], recv_sem=recv.at[own],
                device_id={"gx": (own + 2 * k) % ngx}, device_id_type=MESH,
            )

        def to_partner(block, at, k):
            return pltpu.make_async_remote_copy(
                src_ref=block, dst_ref=slots.at[at], send_sem=send.at[k], recv_sem=recv.at[at],
                device_id={"gx": partner}, device_id_type=MESH,
            )

        def arrived(at):
            pltpu.make_async_remote_copy(
                src_ref=slots.at[at], dst_ref=slots.at[at], send_sem=send.at[0], recv_sem=recv.at[at],
                device_id={"gx": partner}, device_id_type=MESH,
            ).wait_recv()

        def start():
            def go(k, carry):
                direct(k).start()
                return carry

            lax.fori_loop(1, chips, go, 0)
            to_partner(source, own, 0).start()

        def relay():
            def step(k, carry):
                at = (own + ngx - 2 * k) % ngx
                arrived(at)
                to_partner(slots.at[at], at, chips - 1 + k).start()
                return carry

            lax.fori_loop(1, chips, step, 0)

            def rest(k, carry):
                arrived((partner + ngx - 2 * k) % ngx)
                return carry

            lax.fori_loop(0, chips, rest, 0)

        def finish():
            def step(k, carry):
                direct(k).wait_send()
                to_partner(slots.at[own], own, chips - 1 + k).wait_send()
                return carry

            lax.fori_loop(1, chips, step, 0)
            to_partner(source, own, 0).wait_send()

        return start, relay, finish

    start1, relay1, finish1 = gather(vel, i, vg, x_send, x_recv)
    start1()
    pl.semaphore_signal(token, inc=1, device_id={"gy": (j + near) % ngy}, device_id_type=MESH)
    pl.semaphore_signal(token, inc=1, device_id={"gy": (j + ngy - near) % ngy}, device_id_type=MESH)
    b3[...] = jnp.zeros(b3.shape, F32)
    ext[:, 0:8, :] = jnp.zeros((5, 8, 384), F32)
    ext[:, 152:160, :] = jnp.zeros((5, 8, 384), F32)
    copies[0].wait()
    copies[1].wait()
    for v in range(4):
        ext[v, 16:144, 0:256] = acs[v].astype(F32)
    ext[4, 16:144, 0:256] = 1.0 - wls[...].astype(F32)


    def strip(to, rows_from, rows_to, n):
        return pltpu.make_async_remote_copy(
            src_ref=ext.at[:, pl.ds(rows_from, 8), pl.ds(0, 256)],
            dst_ref=ext.at[:, pl.ds(rows_to, 8), pl.ds(0, 256)],
            send_sem=h_send.at[n], recv_sem=h_recv.at[n],
            device_id={"gy": to}, device_id_type=MESH,
        )

    go_down, go_up = strip(down, 136, 8, 0), strip(up, 16, 144, 1)
    go_down.start()
    go_up.start()
    relay1()

    for n in (4, 5, 6):
        copies[n].wait()

    def combine(c, carry):
        rows = pl.ds(pl.multiple_of(8 * c, 8), 8)
        sums = [None] * 6
        for d in range(ngx):
            u, v = vg[d, 0, rows, :], vg[d, 1, rows, :]
            cosine, sine = fxs[d : d + 1, :], fxs[ngx + d : ngx + d + 1, :]
            for f, value in enumerate((u * u, u * v, v * v)):
                real, imag = value * cosine, value * sine
                sums[2 * f] = real if d == 0 else sums[2 * f] + real
                sums[2 * f + 1] = -imag if d == 0 else sums[2 * f + 1] - imag
        for f in range(3):
            zs[f, 0, rows, :] = sums[2 * f]
            zs[f, 1, rows, :] = sums[2 * f + 1]
        return carry

    lax.fori_loop(0, 8, combine, 0)
    w_high, w_low = wxm[0], wxm[1]
    for f in range(3):
        pieces = []
        for real, imag in zip(parts(zs[f, 0]), parts(zs[f, 1])):
            plain = jnp.concatenate([real, imag], axis=1)
            turned = jnp.concatenate([imag, -real], axis=1)
            both = [turned, -plain] if f == 1 else [plain, turned]
            pieces.append(jnp.concatenate(both, axis=0))
        high, low = pieces
        lines = dot_t(w_high, high) + dot_t(w_high, low) + dot_t(w_low, high)
        for s in range(ns):
            b3[pl.ds(ns * f + s, ngy, stride=rpm), :] = lines[ngy * s : ngy * s + ngy]

    def offset(m):
        step = (m + 1) // 2
        return ngy // 2 + jnp.where(m % 2 == 1, step, -step)

    def send3(k):
        to = (j + k) % ngy
        return pltpu.make_async_remote_copy(
            src_ref=b3.at[pl.ds(pl.multiple_of(to * rpm, 8), rpm), :], dst_ref=r3.at[j],
            send_sem=y_send.at[k], recv_sem=y_recv.at[j],
            device_id={"gy": to}, device_id_type=MESH,
        )

    def recv3(d):
        return pltpu.make_async_remote_copy(
            src_ref=r3.at[d], dst_ref=r3.at[d], send_sem=y_send.at[0], recv_sem=y_recv.at[d],
            device_id={"gy": d}, device_id_type=MESH,
        )

    def go3(m, carry):
        send3(offset(m)).start()
        return carry

    pl.semaphore_wait(token, 2)
    lax.fori_loop(0, ngy - 1, go3, 0)
    r3[j] = b3[pl.ds(pl.multiple_of(j * rpm, 8), rpm), :]

    go_down.wait()
    go_up.wait()
    ext[:, 8:16, 0:256] = jnp.where(j > 0, ext[:, 8:16, 0:256], 0.0)
    ext[:, 144:152, 0:256] = jnp.where(j < ngy - 1, ext[:, 144:152, 0:256], 0.0)

    strip_lane = lax.broadcasted_iota(jnp.int32, (144, 128), 1)
    for side in range(2):
        packed = jnp.zeros((144, 128), F32)
        for v in range(5):
            if side == 0:
                moved = pltpu.roll(ext[v, 8:152, 128:256], (8 * v - 120) % 128, 1)
            else:
                moved = pltpu.roll(ext[v, 8:152, 0:128], 8 * v, 1) if v else ext[v, 8:152, 0:128]
            packed = jnp.where((strip_lane >= 8 * v) & (strip_lane < 8 * v + 8), moved, packed)
        xsend[side] = packed

    def column(to, n):
        return pltpu.make_async_remote_copy(
            src_ref=xsend.at[n], dst_ref=xrecv.at[n],
            send_sem=h_send.at[2 + n], recv_sem=h_recv.at[2 + n],
            device_id={"gx": to}, device_id_type=MESH,
        )

    go_right, go_left = column(right, 0), column(left, 1)
    go_right.start()
    go_left.start()

    row = lax.broadcasted_iota(jnp.int32, (rpm, 128), 0)
    lane = lax.broadcasted_iota(jnp.int32, (rpm, 128), 1)
    field, slot = row // ns, row % ns
    wave = i + ngx * (j + ngy * slot)
    is_packed = wave == 0
    in_imag = lane >= 64
    wave_x = jnp.where(is_packed & in_imag, 64 * ngx, wave).astype(F32)

    def coefficients(q, carry):
        index = q + ngy * (lane % 64)
        wave_y = jnp.where(index >= 32 * ngy, index - 64 * ngy, index).astype(F32)
        xx, yy = wave_x * wave_x, wave_y * wave_y
        inverse = -1.0 / jnp.maximum(xx + yy, 1.0)
        k1[q] = jnp.where(field == 0, xx * inverse, jnp.where(field == 2, yy * inverse, 0.0))
        cross = (field == 1) & jnp.logical_not(is_packed) & (index != 32 * ngy)
        k2[q] = jnp.where(cross, 2.0 * wave_x * wave_y * inverse, 0.0)
        return carry

    lax.fori_loop(0, half, coefficients, 0)

    copies[2].wait()
    copies[3].wait()

    def tile_of(ref, column):
        return ref[:, pl.ds(pl.multiple_of(column, 128), 128)]

    narrow = lax.broadcasted_iota(jnp.int32, (4, 128), 1)
    total_x, total_y = 256 * ngx, 128 * ngy
    outer = jnp.where(
        narrow < 64,
        tile_of(wxs, (256 * i + 256) % total_x),
        tile_of(wxs, (256 * i + total_x - 128) % total_x),
    )
    tiles = [tile_of(wxs, 256 * i), tile_of(wxs, 256 * i + 128), outer]
    for t, weights in enumerate(tiles):
        fine = 128 * t + lax.broadcasted_iota(jnp.int32, (256, 128), 1)
        fine = jnp.where(fine < 320, fine, fine - 384) + 16
        coarse = lax.broadcasted_iota(jnp.int32, (256, 128), 0) - 4
        tap = coarse - (fine // 2 - 8 - 1)
        matrix = jnp.zeros((256, 128), F32)
        for s in range(4):
            matrix = matrix + jnp.where(tap == s, weights[s : s + 1, :], 0.0)
        high, low = parts(matrix)
        ax[0, :, 128 * t : 128 * t + 128] = high
        ax[1, :, 128 * t : 128 * t + 128] = low
    outer = jnp.where(
        narrow < 64,
        tile_of(wys, (128 * j + 128) % total_y),
        tile_of(wys, (128 * j + total_y - 128) % total_y),
    )
    for t, weights in enumerate([tile_of(wys, 128 * j), outer]):
        fine = 128 * t + lax.broadcasted_iota(jnp.int32, (128, 128), 1)
        fine = jnp.where(fine < 192, fine, fine - 256) + 16
        coarse = lax.broadcasted_iota(jnp.int32, (128, 128), 0) - 4
        tap = coarse - (fine // 2 - 8 - 1)
        matrix = jnp.zeros((128, 128), F32)
        for s in range(4):
            matrix = matrix + jnp.where(tap == s, weights[s : s + 1, :], 0.0)
        high, low = parts(jnp.transpose(matrix))
        ay[0, 128 * t : 128 * t + 128, :] = high
        ay[1, 128 * t : 128 * t + 128, :] = low

    go_right.wait()
    go_left.wait()
    for v in range(5):
        from_right = pltpu.roll(xrecv[1], (-8 * v) % 128, 1) if v else xrecv[1]
        from_left = pltpu.roll(xrecv[0], 120 - 8 * v, 1)
        from_right = jnp.where((strip_lane < 8) & (i < ngx - 1), from_right, 0.0)
        ext[v, 8:152, 256:384] = jnp.where((strip_lane >= 120) & (i > 0), from_left, from_right)

    def rates(planes, at, rows):
        here = pl.ds(at, rows)
        window = pl.ds(pl.multiple_of(at - 8, 8), rows + 16)
        b_window, p_window = planes[2, window, :], planes[3, window, :]
        b, p = b_window[8 : 8 + rows], p_window[8 : 8 + rows]
        rho, a = planes[0, here, :], planes[1, here, :]
        slope_b, slope_p = slope_y(b_window, rows), slope_y(p_window, rows)
        return (
            (rho, slope_x(a + 0.3 * rho) + slope_b),
            (a, slope_x(p + 0.3 * a)),
            (b, slope_x(0.3 * b) + slope_p),
            (p, slope_x(a + 0.3 * p) + slope_b),
        )

    def stage_one(c, carry):
        at = pl.multiple_of(8 + 8 * c, 8)
        here = pl.ds(at, 8)
        open_cells = ext[4, here, :]
        for v, (value, rate) in enumerate(rates(ext, at, 8)):
            mid[v, here, :] = open_cells * (value - 0.5 * rate)
            adv[v, here, :] = (value - 0.25 * rate)[:, 0:256]
        return carry

    lax.fori_loop(0, 18, stage_one, 0)

    def got3(k, carry):
        recv3((j + k) % ngy).wait_recv()
        return carry

    for n in range(7, 13):
        copies[n].wait()
    lax.fori_loop(1, ngy, got3, 0)

    spectrum = rfft([r3[d] for d in range(ngy)])
    for q, (real, imag) in enumerate(spectrum):
        rows = slice(rpm * q, rpm * q + rpm)
        cosine, sine = twfs[0, q : q + 1, :], twfs[1, q : q + 1, :]
        if imag is None:
            gs[rows, 0:128] = real * cosine
            gs[rows, 128:256] = -(real * sine)
        else:
            gs[rows, 0:128] = real * cosine + imag * sine
            gs[rows, 128:256] = imag * cosine - real * sine
    gs[...] = dot3(parts(gs[...]), (yfs[0], yfs[1]))
    corner = (row == ns) & (lane == 96) & (i == 0) & (j == 0)
    row_lane = lax.broadcasted_iota(jnp.int32, (ns, 128), 1)
    for q in range(half):
        real, imag = gs[rpm * q : rpm * q + rpm, 0:128], gs[rpm * q : rpm * q + rpm, 128:256]
        total_real = k1[q] * real - k2[q] * imag
        total_imag = k1[q] * imag + k2[q] * real
        if q == 0:
            total_real = total_real - jnp.where(corner, pltpu.roll(real, 64, 1), 0.0)
            total_imag = total_imag - jnp.where(corner, pltpu.roll(imag, 64, 1), 0.0)
        for n, total in enumerate((total_real, total_imag)):
            value = total[0:ns] + total[ns : 2 * ns] + total[2 * ns : 3 * ns]
            lanes = slice(128 * n, 128 * n + 128)
            at = 2 * ns * q
            ps[at : at + ns, lanes] = jnp.where(row_lane < 64, value, 0.0)
            ps[at + ns : at + 2 * ns, lanes] = jnp.where(row_lane < 64, 0.0, value)
    us[...] = dot3(parts(ps[...]), (yis[0], yis[1]))
    terms = []
    for q in range(half):
        rows = slice(2 * ns * q, 2 * ns * q + 2 * ns)
        real, imag = us[rows, 0:128], us[rows, 128:256]
        cosine, sine = twis[0, q : q + 1, :], twis[1, q : q + 1, :]
        turned_real = real * cosine - imag * sine
        if q in (0, half - 1):
            terms.append((turned_real, None))
        else:
            terms.append((turned_real, real * sine + imag * cosine))
    for d, value in enumerate(real_sum(terms)):
        b4[d] = value

    def send4(k):
        to = (j + k) % ngy
        return pltpu.make_async_remote_copy(
            src_ref=b4.at[to], dst_ref=r4.at[j], send_sem=v_send.at[k], recv_sem=v_recv.at[j],
            device_id={"gy": to}, device_id_type=MESH,
        )

    def recv4(d):
        return pltpu.make_async_remote_copy(
            src_ref=r4.at[d], dst_ref=r4.at[d], send_sem=v_send.at[0], recv_sem=v_recv.at[d],
            device_id={"gy": d}, device_id_type=MESH,
        )

    def go4(m, carry):
        send4(offset(m)).start()
        return carry

    def got4(k, carry):
        recv4((j + k) % ngy).wait_recv()
        return carry

    lax.fori_loop(0, ngy - 1, go4, 0)
    r4[j] = b4[j]

    def stage_two(c, carry):
        at = pl.multiple_of(16 + 8 * c, 8)
        here = pl.ds(at, 8)
        open_cells = ext[4, here, 0:256]
        for v, (value, rate) in enumerate(rates(mid, at, 8)):
            adv[v, here, :] = open_cells * (adv[v, here, :] - 0.25 * rate[:, 0:256])
        return carry

    lax.fori_loop(0, 16, stage_two, 0)

    lax.fori_loop(1, ngy, got4, 0)
    for g in range(ngy):
        s4[2 * ns * g : 2 * ns * g + 2 * ns, :] = r4[g]
    sb[...] = jnp.transpose(s4[...])[0:PX]
    start2, relay2, finish2 = gather(sb, i, sg, w_send, w_recv)
    start2()
    sg[i] = sb[...]
    relay2()

    pressure = jnp.zeros((PX, 256), F32)
    blocks = [(0, 1, 1)] + [(a, min(a + 5, ngx), 0) for a in range(1, ngx, 5)]
    for begin, end, variant in blocks:
        lines = sg[begin:end].reshape((end - begin) * PX, 128)
        mixed = dot3(parts(lines), (dxs[variant, 0], dxs[variant, 1]))
        for n in range(begin, end):
            rows = slice((n - begin) * PX, (n - begin + 1) * PX)
            cosine, sine = cxs[n : n + 1, :], cxs[ngx + n : ngx + n + 1, :]
            pressure = pressure + (mixed[rows, 0:256] * cosine - mixed[rows, 256:512] * sine)

    along = dot3(parts(pressure), (ax[0], ax[1]))
    along = jnp.concatenate([along, jnp.zeros((128 - PX, 384), F32)], axis=0)
    source = dot3((ay[0], ay[1]), parts(along))
    qs[16:152, :] = 0.5 * ext[4, 16:152, :] * source[0:136]
    qs[8:16, :] = 0.5 * ext[4, 8:16, :] * source[248:256]
    qs[0:8, :] = jnp.zeros((8, 384), F32)
    qs[152:160, :] = jnp.zeros((8, 384), F32)

    def last(c, carry):
        at = pl.multiple_of(16 + 16 * c, 16)
        here = pl.ds(at, 16)
        there = pl.ds(pl.multiple_of(16 * c, 16), 16)
        window = qs[pl.ds(pl.multiple_of(at - 8, 8), 32), :]
        half_source = window[8:24]
        quarter = 0.25 * ext[4, here, 0:256]
        change_x = quarter * slope_x(half_source)[:, 0:256]
        change_y = quarter * slope_y(window, 16)[:, 0:256]
        out[0, there, :] = adv[0, here, :].astype(BF16)
        out[1, there, :] = (adv[1, here, :] - change_x).astype(BF16)
        out[2, there, :] = (adv[2, here, :] - change_y).astype(BF16)
        out[3, there, :] = (adv[3, here, :] + half_source[:, 0:256] - 0.3 * change_x).astype(BF16)
        return carry

    lax.fori_loop(0, 8, last, 0)

    finish1()
    finish2()

    def left3(k, carry):
        send3(k).wait_send()
        return carry

    def left4(k, carry):
        send4(k).wait_send()
        return carry

    lax.fori_loop(1, ngy, left3, 0)
    lax.fori_loop(1, ngy, left4, 0)


def solution(mesh):
    ngx, ngy = mesh.shape["gx"], mesh.shape["gy"]
    ns, half = 64 // ngy, ngy // 2 + 1
    rpm = max(8, 3 * ns)
    consts = tables(ngx, ngy)

    def shards(velocity, weights_x, weights_y, acoustic, wall_mask):
        vel = velocity.reshape(2, 64, 128)
        ac = acoustic.reshape(4, 128, 256)
        wall = wall_mask.reshape(128, 256)
        fx, wx, twf, yf, twi, yi, dx, cx = [jnp.asarray(c) for c in consts]
        anywhere = pl.BlockSpec(memory_space=pl.ANY)
        vmem = pltpu.VMEM
        dma = pltpu.SemaphoreType.DMA
        scratch = [
            vmem((ngx, 2, 64, 128), F32),
            vmem((4, 128, 256), BF16),
            vmem((128, 256), jnp.int32),
            vmem((4, 256 * ngx), F32),
            vmem((4, 128 * ngy), F32),
            vmem(fx.shape[1:], F32),
            vmem(wx.shape[1:], BF16),
            vmem(twf.shape, F32),
            vmem(yf.shape, BF16),
            vmem(twi.shape, F32),
            vmem(yi.shape, BF16),
            vmem(dx.shape, BF16),
            vmem(cx.shape[1:], F32),
            vmem((5, 160, 384), F32),
            vmem((4, 160, 384), F32),
            vmem((4, 160, 256), F32),
            vmem((2, 144, 128), F32),
            vmem((2, 144, 128), F32),
            vmem((2, 256, 384), BF16),
            vmem((2, 256, 128), BF16),
            vmem((half, rpm, 128), F32),
            vmem((half, rpm, 128), F32),
            vmem((3, 2, 64, 128), F32),
            vmem((ngy * rpm, 128), F32),
            vmem((ngy, rpm, 128), F32),
            vmem((half * rpm, 256), F32),
            vmem((half * 2 * ns, 256), F32),
            vmem((half * 2 * ns, 256), F32),
            vmem((ngy, 2 * ns, 128), F32),
            vmem((ngy, 2 * ns, 128), F32),
            vmem((128, 128), F32),
            vmem((PX, 128), F32),
            vmem((ngx, PX, 128), F32),
            vmem((160, 384), F32),
            dma((13,)),
            dma((ngx,)), dma((ngx,)),
            dma((ngy,)), dma((ngy,)),
            dma((4,)), dma((4,)),
            dma((ngy,)), dma((ngy,)),
            dma((ngx,)), dma((ngx,)),
            pltpu.SemaphoreType.REGULAR,
        ]
        result = pl.pallas_call(
            functools.partial(kernel, ngx, ngy),
            out_shape=jax.ShapeDtypeStruct((4, 128, 256), BF16),
            in_specs=[anywhere] * 13,
            out_specs=pl.BlockSpec(memory_space=pltpu.VMEM),
            scratch_shapes=scratch,
            compiler_params=pltpu.CompilerParams(
                collective_id=0, has_side_effects=True
            ),
            name="poisson_step",
        )(vel, weights_x, weights_y, ac, wall, fx, wx, twf, yf, twi, yi, dx, cx)
        return result.reshape(4, 1, 128, 256)

    in_specs = (P(None, None, "gy", "gx"), P(), P(), P(None, None, "gy", "gx"), P(None, "gy", "gx"))
    return jax.shard_map(
        shards, mesh=mesh, in_specs=in_specs, out_specs=P(None, None, "gy", "gx"), check_vma=False
    )
```

```python
import functools
import math

import jax
import jax.numpy as jnp
import numpy as np
from jax import lax
from jax.experimental import pallas as pl
from jax.experimental.pallas import tpu as pltpu
from jax.sharding import PartitionSpec as P

F32 = jnp.float32
BF16 = jnp.bfloat16
MESH = pl.DeviceIdType.MESH
PX = 72


def two_parts(array):
    high = array.astype(BF16)
    low = (array - high.astype(np.float64)).astype(BF16)
    return np.stack([high, low])


def turn(products, modulus):
    return 2.0 * np.pi / modulus * np.mod(products, modulus).astype(np.float64)


@functools.lru_cache(maxsize=None)
def tables(ngx, ngy):
    nx, ny, ns, half = 128 * ngx, 64 * ngy, 64 // ngy, ngy // 2 + 1
    lane = np.arange(128)
    wide = np.arange(256) - 4
    order = np.concatenate([np.arange(0, ngx, 2), np.arange(1, ngx, 2)])
    place = (128 * order[:, None] + lane)[None] * np.arange(ngx)[:, None, None]
    angle = turn(place, nx)
    fx = np.concatenate([np.cos(angle), np.sin(angle)], axis=1).astype(np.float32)
    angle = turn(np.arange(64)[:, None] * lane[None], 128)
    wx = two_parts(np.concatenate([np.cos(angle), np.sin(angle)], axis=1))
    sums = np.zeros((8, 128), dtype=BF16)
    sums[0], sums[1] = 1.0, (-1.0) ** lane
    angle = turn(np.arange(half)[:, None] * (lane % 64)[None], ny)
    twf = np.stack([np.cos(angle), np.sin(angle)]).astype(np.float32)
    angle = turn(np.arange(64)[:, None] * np.arange(64)[None], 64)
    cos2 = np.kron(np.eye(2), np.cos(angle))
    sin2 = np.kron(np.eye(2), np.sin(angle))
    yf = two_parts(np.block([[cos2, -sin2], [sin2, cos2]]))
    angle = turn(np.arange(64)[:, None] * (lane - 4)[None], 64)
    cos2 = np.concatenate([np.cos(angle)] * 2)
    sin2 = np.concatenate([np.sin(angle)] * 2)
    yi = two_parts(np.block([[cos2, sin2], [-sin2, cos2]]))
    angle = turn(np.arange(half)[:, None] * (lane - 4)[None], ny)
    scale = np.full((half, 1), 2.0)
    scale[0] = scale[-1] = 1.0
    scale = scale / (nx * ny)
    twi = np.stack([scale * np.cos(angle), scale * np.sin(angle)]).astype(np.float32)
    k2 = np.arange(ngy)[:, None] + ngy * np.arange(ns)[None]
    angle = turn(k2[..., None] * wide, 128)
    cosine, sine = 2.0 * np.cos(angle), 2.0 * np.sin(angle)
    rows = np.zeros((ngy, 2, ns, 512))
    rows[:, 0, :, :256], rows[:, 0, :, 256:] = cosine, sine
    rows[:, 1, :, :256], rows[:, 1, :, 256:] = -sine, cosine
    dx = two_parts(rows.reshape(128, 512))
    place = (128 * np.arange(ngx)[:, None] + wide)[:, None, :] * order[None, :, None]
    angle = turn(place, nx)
    cx = np.concatenate([np.cos(angle), np.sin(angle)], axis=1).astype(np.float32)
    return fx, wx, sums, twf, yf, twi, yi, dx, cx


def rfft(values):
    count = len(values)
    if count == 1:
        return [(values[0], None)]
    even, odd = rfft(values[0::2]), rfft(values[1::2])
    if count == 2:
        return [(even[0][0] + odd[0][0], None), (even[0][0] - odd[0][0], None)]
    middle = count // 2

    def full(half, k):
        k = k % middle
        if k <= middle // 2:
            return half[k]
        real, imag = half[middle - k]
        return (real, None if imag is None else -imag)

    result = []
    for k in range(middle + 1):
        er, ei = full(even, k)
        orr, oi = full(odd, k)
        if k == 0:
            result.append((er + orr, None))
        elif k == middle:
            result.append((er - orr, None))
        elif 2 * k == middle:
            result.append((er, -orr))
        else:
            c, s = math.cos(2 * math.pi * k / count), math.sin(2 * math.pi * k / count)
            tr = c * orr + (0.0 if oi is None else s * oi)
            ti = (0.0 if oi is None else c * oi) - s * orr
            result.append((er + tr, ti if ei is None else ei + ti))
    return result


def real_sum(spectrum):
    middle = len(spectrum) - 1
    if middle == 1:
        a, b = spectrum[0][0], spectrum[1][0]
        return [a + b, a - b]
    count = 2 * middle

    def fold(values):
        folded = []
        for k in range(middle // 2 + 1):
            if 2 * k == middle:
                folded.append((values[k][0], None))
                continue
            ar, ai = values[k]
            br, bi = values[middle - k]
            if k == 0:
                folded.append((ar + br, None))
            else:
                folded.append((ar + br, ai - bi))
        return folded

    twisted = []
    for k in range(middle + 1):
        vr, vi = spectrum[k]
        if k == 0:
            twisted.append((vr, None))
        elif k == middle:
            twisted.append((-vr, None))
        elif 2 * k == middle:
            twisted.append((-vi, vr))
        else:
            c, s = math.cos(2 * math.pi * k / count), math.sin(2 * math.pi * k / count)
            twisted.append((c * vr - s * vi, c * vi + s * vr))
    even, odd = real_sum(fold(spectrum)), real_sum(fold(twisted))
    result = []
    for a, b in zip(even, odd):
        result += [a, b]
    return result


def parts(value):
    high = value.astype(BF16)
    return high, (value - high.astype(F32)).astype(BF16)


def dot(a, b):
    return jnp.dot(a, b, preferred_element_type=F32)


def dot3(left, right):
    lh, ll = left
    rh, rl = right
    return dot(lh, rh) + dot(lh, rl) + dot(ll, rh)


def dot_t(a, b):
    return lax.dot_general(a, b, (((1,), (1,)), ((), ())), preferred_element_type=F32)


def shifted(value, step):
    width = value.shape[-1]
    return pltpu.roll(value, (-step) % width, value.ndim - 1)


WEIGHTS = (0.75, -0.15, 1.0 / 60.0)


def slope_x(value):
    total = None
    for index, weight in enumerate(WEIGHTS):
        term = weight * (shifted(value, index + 1) - shifted(value, -index - 1))
        total = term if total is None else total + term
    return total


def slope_y(window, rows):
    total = None
    for index, weight in enumerate(WEIGHTS):
        k = index + 1
        term = weight * (window[8 + k : 8 + k + rows] - window[8 - k : 8 - k + rows])
        total = term if total is None else total + term
    return total


def kernel(
    ngx, ngy,
    vel, weights_x, weights_y, ac, wall, fx, wx, sums, twf, yf, twi, yi, dx, cx,
    out,
    vg, acs, wls, wxs, wys, fxs, wxm, sms, twfs, yfs, twis, yis, dxs, cxs,
    ext, mid, adv, xsend, xrecv, ax, ay, k1, k2,
    zs, b2, b3, r3, gs, ps, us, b4, r4, s4, sb, sg, pacc, qs, es, ob,
    loc, x_send, x_recv, y_send, y_recv, h_send, h_recv, v_send, v_recv, w_send, w_recv, e_send, e_recv, o_sem, token,
):
    ns, half = 64 // ngy, ngy // 2 + 1
    rpm = 2 * ns
    i, j = lax.axis_index("gx"), lax.axis_index("gy")
    partner = i + 1 - 2 * (i % 2)
    right, left = (i + 1) % ngx, (i + ngx - 1) % ngx
    down, up = (j + 1) % ngy, (j + ngy - 1) % ngy
    chips = ngx // 2

    barrier = pltpu.get_barrier_semaphore()
    near = ngy // 4

    def greet_y(k, carry):
        pl.semaphore_signal(barrier, inc=1, device_id={"gy": (j + k) % ngy}, device_id_type=MESH)
        pl.semaphore_signal(
            barrier, inc=1, device_id={"gy": (j + ngy - k) % ngy}, device_id_type=MESH
        )
        return carry

    def greet_x(k, carry):
        pl.semaphore_signal(barrier, inc=1, device_id={"gx": (i + 2 * k) % ngx}, device_id_type=MESH)
        return carry

    lax.fori_loop(1, near + 1, greet_y, 0)
    lax.fori_loop(1, chips, greet_x, 0)
    pl.semaphore_signal(barrier, inc=1, device_id={"gx": right}, device_id_type=MESH)
    pl.semaphore_signal(barrier, inc=1, device_id={"gx": left}, device_id_type=MESH)

    parity = i % 2
    place = parity * chips + i // 2
    sources = [
        (ac, acs), (wall, wls), (weights_x, wxs), (weights_y, wys), (vel, vg.at[place]),
        (fx.at[i], fxs), (wx, wxm), (sums, sms), (twf, twfs), (yf, yfs), (twi, twis), (yi, yis),
        (dx, dxs), (cx.at[i], cxs),
    ]
    copies = [pltpu.make_async_copy(a, b, loc.at[n]) for n, (a, b) in enumerate(sources)]
    for copy in copies:
        copy.start()

    pl.semaphore_wait(barrier, 2 * near + chips - 1 + 2)

    def slot_of(k):
        return (k % 2) * chips + k // 2

    def gather(source, own, slots, send, recv):
        mine = slot_of(own)

        def direct(k):
            return pltpu.make_async_remote_copy(
                src_ref=source, dst_ref=slots.at[mine], send_sem=send.at[k], recv_sem=recv.at[mine],
                device_id={"gx": (own + 2 * k) % ngx}, device_id_type=MESH,
            )

        def to_partner(block, at, k):
            return pltpu.make_async_remote_copy(
                src_ref=block, dst_ref=slots.at[at], send_sem=send.at[k], recv_sem=recv.at[at],
                device_id={"gx": partner}, device_id_type=MESH,
            )

        def arrived(at):
            pltpu.make_async_remote_copy(
                src_ref=slots.at[at], dst_ref=slots.at[at], send_sem=send.at[0], recv_sem=recv.at[at],
                device_id={"gx": partner}, device_id_type=MESH,
            ).wait_recv()

        def start():
            def go(k, carry):
                direct(k).start()
                return carry

            lax.fori_loop(1, chips, go, 0)
            to_partner(source, mine, 0).start()

        def relay():
            def step(k, carry):
                at = slot_of((own + ngx - 2 * k) % ngx)
                arrived(at)
                to_partner(slots.at[at], at, chips - 1 + k).start()
                return carry

            lax.fori_loop(1, chips, step, 0)

        def rest():
            def step(k, carry):
                arrived(slot_of((partner + ngx - 2 * k) % ngx))
                return carry

            lax.fori_loop(0, chips, step, 0)

        def finish():
            def step(k, carry):
                direct(k).wait_send()
                to_partner(slots.at[mine], mine, chips - 1 + k).wait_send()
                return carry

            lax.fori_loop(1, chips, step, 0)
            to_partner(source, mine, 0).wait_send()

        return start, relay, rest, finish

    start1, relay1, rest1, finish1 = gather(vel, i, vg, x_send, x_recv)
    start1()
    pl.semaphore_signal(token, inc=1, device_id={"gy": (j + near) % ngy}, device_id_type=MESH)
    pl.semaphore_signal(token, inc=1, device_id={"gy": (j + ngy - near) % ngy}, device_id_type=MESH)
    ext[:, 0:8, :] = jnp.zeros((5, 8, 384), F32)
    ext[:, 152:160, :] = jnp.zeros((5, 8, 384), F32)
    copies[0].wait()
    copies[1].wait()
    for v in range(4):
        ext[v, 16:144, 0:256] = acs[v].astype(F32)
    ext[4, 16:144, 0:256] = 1.0 - wls[...].astype(F32)


    def strip(to, rows_from, rows_to, n):
        return pltpu.make_async_remote_copy(
            src_ref=ext.at[:, pl.ds(rows_from, 8), pl.ds(0, 256)],
            dst_ref=ext.at[:, pl.ds(rows_to, 8), pl.ds(0, 256)],
            send_sem=h_send.at[n], recv_sem=h_recv.at[n],
            device_id={"gy": to}, device_id_type=MESH,
        )

    go_down, go_up = strip(down, 136, 8, 0), strip(up, 16, 144, 1)
    go_down.start()
    go_up.start()
    relay1()
    for n in (4, 5, 6, 7):
        copies[n].wait()

    def combine(half_at, begin):
        def step(c, carry):
            rows = pl.ds(pl.multiple_of(8 * c, 8), 8)
            total = [None] * 5 if begin else [zs[n, rows, :] for n in range(5)]
            for m in range(chips):
                u, v = vg[half_at + m, 0, rows, :], vg[half_at + m, 1, rows, :]
                cosine = fxs[pl.ds(half_at + m, 1), :]
                sine = fxs[pl.ds(ngx + half_at + m, 1), :]
                uu, vv, uv = u * u, v * v, u * v
                difference = uu - vv
                terms = (
                    difference * cosine, -(difference * sine), uv * cosine, -(uv * sine),
                    0.5 * (uu + vv),
                )
                total = [b if a is None else a + b for a, b in zip(total, terms)]
            for n in range(5):
                zs[n, rows, :] = total[n]
            return carry

        lax.fori_loop(0, 8, step, 0)

    combine(parity * chips, True)
    rest1()
    combine(chips - parity * chips, False)
    w_high, w_low = wxm[0], wxm[1]
    for f in range(2):
        pieces = []
        for real, imag in zip(parts(zs[2 * f]), parts(zs[2 * f + 1])):
            plain = jnp.concatenate([real, imag], axis=1)
            turned = jnp.concatenate([imag, -real], axis=1)
            both = [turned, -plain] if f == 1 else [plain, turned]
            pieces.append(jnp.concatenate(both, axis=0))
        high, low = pieces
        lines = dot_t(w_high, high) + dot_t(w_high, low) + dot_t(w_low, high)
        for s in range(ns):
            b2[pl.ds(ns * f + s, ngy, stride=rpm), :] = lines[ngy * s : ngy * s + ngy]
    alternating, plain_sum = [], None
    for n in (0, 2, 4):
        high, low = parts(zs[n])
        row_sums = dot_t(sms[...], high) + dot_t(sms[...], low)
        if n == 4:
            plain_sum = row_sums[0:1]
        else:
            alternating.append(row_sums[1:2])
    b2[0:1, 64:128] = jnp.where(i == 0, alternating[0], b2[0:1, 64:128])
    b2[ns : ns + 1, 0:64] = jnp.where(i == 0, alternating[1], b2[ns : ns + 1, 0:64])
    b2[ns : ns + 1, 64:128] = jnp.where(i == 0, plain_sum, b2[ns : ns + 1, 64:128])
    for g in range(ngy):
        b3[g] = b2[rpm * g : rpm * g + rpm, :]

    def offset(m):
        step = (m + 1) // 2
        return ngy // 2 + jnp.where(m % 2 == 1, step, -step)

    def send3(k):
        to = (j + k) % ngy
        return pltpu.make_async_remote_copy(
            src_ref=b3.at[to], dst_ref=r3.at[j],
            send_sem=y_send.at[k], recv_sem=y_recv.at[j],
            device_id={"gy": to}, device_id_type=MESH,
        )

    def recv3(d):
        return pltpu.make_async_remote_copy(
            src_ref=r3.at[d], dst_ref=r3.at[d], send_sem=y_send.at[0], recv_sem=y_recv.at[d],
            device_id={"gy": d}, device_id_type=MESH,
        )

    def go3(m, carry):
        send3(offset(m)).start()
        return carry

    pl.semaphore_wait(token, 2)
    lax.fori_loop(0, ngy - 1, go3, 0)
    r3[j] = b3[j]

    go_down.wait()
    go_up.wait()
    ext[:, 8:16, 0:256] = jnp.where(j > 0, ext[:, 8:16, 0:256], 0.0)
    ext[:, 144:152, 0:256] = jnp.where(j < ngy - 1, ext[:, 144:152, 0:256], 0.0)

    strip_lane = lax.broadcasted_iota(jnp.int32, (144, 128), 1)
    for side in range(2):
        packed = jnp.zeros((144, 128), F32)
        for v in range(5):
            if side == 0:
                moved = pltpu.roll(ext[v, 8:152, 128:256], (8 * v - 120) % 128, 1)
            else:
                moved = pltpu.roll(ext[v, 8:152, 0:128], 8 * v, 1) if v else ext[v, 8:152, 0:128]
            packed = jnp.where((strip_lane >= 8 * v) & (strip_lane < 8 * v + 8), moved, packed)
        xsend[side] = packed

    def column(to, n):
        return pltpu.make_async_remote_copy(
            src_ref=xsend.at[n], dst_ref=xrecv.at[n],
            send_sem=h_send.at[2 + n], recv_sem=h_recv.at[2 + n],
            device_id={"gx": to}, device_id_type=MESH,
        )

    go_right, go_left = column(right, 0), column(left, 1)
    go_right.start()
    go_left.start()

    row = lax.broadcasted_iota(jnp.int32, (rpm, 128), 0)
    lane = lax.broadcasted_iota(jnp.int32, (rpm, 128), 1)
    field, slot = row // ns, row % ns
    wave = i + ngx * (j + ngy * slot)
    is_packed = wave == 0
    in_imag = lane >= 64
    wave_x = jnp.where(is_packed & in_imag, 64 * ngx, wave).astype(F32)

    def coefficients(q, carry):
        index = q + ngy * (lane % 64)
        wave_y = jnp.where(index >= 32 * ngy, index - 64 * ngy, index).astype(F32)
        xx, yy = wave_x * wave_x, wave_y * wave_y
        inverse = -1.0 / jnp.maximum(xx + yy, 1.0)
        k1[q] = jnp.where(field == 0, 0.5 * (xx - yy) * inverse, 0.0)
        cross = (field == 1) & jnp.logical_not(is_packed) & (index != 32 * ngy)
        k2[q] = jnp.where(cross, 2.0 * wave_x * wave_y * inverse, 0.0)
        return carry

    lax.fori_loop(0, half, coefficients, 0)

    copies[2].wait()
    copies[3].wait()

    def tile_of(ref, column):
        return ref[:, pl.ds(pl.multiple_of(column, 128), 128)]

    narrow = lax.broadcasted_iota(jnp.int32, (4, 128), 1)
    total_x, total_y = 256 * ngx, 128 * ngy
    outer = jnp.where(
        narrow < 64,
        tile_of(wxs, (256 * i + 256) % total_x),
        tile_of(wxs, (256 * i + total_x - 128) % total_x),
    )
    tiles = [tile_of(wxs, 256 * i), tile_of(wxs, 256 * i + 128), outer]
    for t, weights in enumerate(tiles):
        fine = 128 * t + lax.broadcasted_iota(jnp.int32, (256, 128), 1)
        fine = jnp.where(fine < 320, fine, fine - 384) + 16
        coarse = lax.broadcasted_iota(jnp.int32, (256, 128), 0) - 4
        tap = coarse - (fine // 2 - 8 - 1)
        matrix = jnp.zeros((256, 128), F32)
        for s in range(4):
            matrix = matrix + jnp.where(tap == s, weights[s : s + 1, :], 0.0)
        high, low = parts(matrix)
        ax[0, :, 128 * t : 128 * t + 128] = high
        ax[1, :, 128 * t : 128 * t + 128] = low
    outer = jnp.where(
        narrow < 64,
        tile_of(wys, (128 * j + 128) % total_y),
        tile_of(wys, (128 * j + total_y - 128) % total_y),
    )
    for t, weights in enumerate([tile_of(wys, 128 * j), outer]):
        fine = 128 * t + lax.broadcasted_iota(jnp.int32, (128, 128), 1)
        fine = jnp.where(fine < 192, fine, fine - 256) + 16
        coarse = lax.broadcasted_iota(jnp.int32, (128, 128), 0) - 4
        tap = coarse - (fine // 2 - 8 - 1)
        matrix = jnp.zeros((128, 128), F32)
        for s in range(4):
            matrix = matrix + jnp.where(tap == s, weights[s : s + 1, :], 0.0)
        high, low = parts(jnp.transpose(matrix))
        ay[0, 128 * t : 128 * t + 128, :] = high
        ay[1, 128 * t : 128 * t + 128, :] = low

    go_right.wait()
    go_left.wait()
    for v in range(5):
        from_right = pltpu.roll(xrecv[1], (-8 * v) % 128, 1) if v else xrecv[1]
        from_left = pltpu.roll(xrecv[0], 120 - 8 * v, 1)
        from_right = jnp.where((strip_lane < 8) & (i < ngx - 1), from_right, 0.0)
        ext[v, 8:152, 256:384] = jnp.where((strip_lane >= 120) & (i > 0), from_left, from_right)

    def rates(planes, at, rows):
        here = pl.ds(at, rows)
        window = pl.ds(pl.multiple_of(at - 8, 8), rows + 16)
        b_window, p_window = planes[2, window, :], planes[3, window, :]
        b, p = b_window[8 : 8 + rows], p_window[8 : 8 + rows]
        rho, a = planes[0, here, :], planes[1, here, :]
        slope_b, slope_p = slope_y(b_window, rows), slope_y(p_window, rows)
        return (
            (rho, slope_x(a + 0.3 * rho) + slope_b),
            (a, slope_x(p + 0.3 * a)),
            (b, slope_x(0.3 * b) + slope_p),
            (p, slope_x(a + 0.3 * p) + slope_b),
        )

    def stage_one(c, carry):
        at = pl.multiple_of(8 + 8 * c, 8)
        here = pl.ds(at, 8)
        open_cells = ext[4, here, :]
        for v, (value, rate) in enumerate(rates(ext, at, 8)):
            mid[v, here, :] = open_cells * (value - 0.5 * rate)
            adv[v, here, :] = (value - 0.25 * rate)[:, 0:256]
        return carry

    lax.fori_loop(0, 18, stage_one, 0)

    energies = []
    for block in (left, i, right):
        u, v = vg[slot_of(block), 0], vg[slot_of(block), 1]
        energies.append(pltpu.roll(0.5 * (u * u + v * v), 4, 1))
    edge = lax.broadcasted_iota(jnp.int32, (64, 128), 1) < 4
    es[8:72, 0:128] = jnp.where(edge, energies[0], energies[1])
    es[8:72, 128:256] = jnp.where(edge, energies[1], energies[2])

    def border(to, rows_from, rows_to, n):
        return pltpu.make_async_remote_copy(
            src_ref=es.at[pl.ds(rows_from, 8), :], dst_ref=es.at[pl.ds(rows_to, 8), :],
            send_sem=e_send.at[n], recv_sem=e_recv.at[n],
            device_id={"gy": to}, device_id_type=MESH,
        )

    border_down, border_up = border(down, 64, 0, 0), border(up, 8, 72, 1)
    border_down.start()
    border_up.start()

    def got3(k, carry):
        recv3((j + k) % ngy).wait_recv()
        return carry

    for n in range(8, 14):
        copies[n].wait()
    lax.fori_loop(1, ngy, got3, 0)

    spectrum = rfft([r3[d] for d in range(ngy)])
    for q, (real, imag) in enumerate(spectrum):
        rows = slice(rpm * q, rpm * q + rpm)
        cosine, sine = twfs[0, q : q + 1, :], twfs[1, q : q + 1, :]
        if imag is None:
            gs[rows, 0:128] = real * cosine
            gs[rows, 128:256] = -(real * sine)
        else:
            gs[rows, 0:128] = real * cosine + imag * sine
            gs[rows, 128:256] = imag * cosine - real * sine
    gs[...] = dot3(parts(gs[...]), (yfs[0], yfs[1]))
    origin = (row == ns) & (i == 0) & (j == 0)
    corner = jnp.where(origin & (lane == 0), 1.0, jnp.where(origin & (lane == 96), -1.0, 0.0))
    row_lane = lax.broadcasted_iota(jnp.int32, (ns, 128), 1)
    for q in range(half):
        real, imag = gs[rpm * q : rpm * q + rpm, 0:128], gs[rpm * q : rpm * q + rpm, 128:256]
        total_real = k1[q] * real - k2[q] * imag
        total_imag = k1[q] * imag + k2[q] * real
        if q == 0:
            total_real = total_real + corner * pltpu.roll(real, 64, 1)
            total_imag = total_imag + corner * pltpu.roll(imag, 64, 1)
        for n, total in enumerate((total_real, total_imag)):
            value = total[0:ns] + total[ns : 2 * ns]
            lanes = slice(128 * n, 128 * n + 128)
            at = 2 * ns * q
            ps[at : at + ns, lanes] = jnp.where(row_lane < 64, value, 0.0)
            ps[at + ns : at + 2 * ns, lanes] = jnp.where(row_lane < 64, 0.0, value)
    us[...] = dot3(parts(ps[...]), (yis[0], yis[1]))
    terms = []
    for q in range(half):
        rows = slice(2 * ns * q, 2 * ns * q + 2 * ns)
        real, imag = us[rows, 0:128], us[rows, 128:256]
        cosine, sine = twis[0, q : q + 1, :], twis[1, q : q + 1, :]
        turned_real = real * cosine - imag * sine
        if q in (0, half - 1):
            terms.append((turned_real, None))
        else:
            terms.append((turned_real, real * sine + imag * cosine))
    for d, value in enumerate(real_sum(terms)):
        b4[d] = value

    def send4(k):
        to = (j + k) % ngy
        return pltpu.make_async_remote_copy(
            src_ref=b4.at[to], dst_ref=r4.at[j], send_sem=v_send.at[k], recv_sem=v_recv.at[j],
            device_id={"gy": to}, device_id_type=MESH,
        )

    def recv4(d):
        return pltpu.make_async_remote_copy(
            src_ref=r4.at[d], dst_ref=r4.at[d], send_sem=v_send.at[0], recv_sem=v_recv.at[d],
            device_id={"gy": d}, device_id_type=MESH,
        )

    def go4(m, carry):
        send4(offset(m)).start()
        return carry

    def got4(k, carry):
        recv4((j + k) % ngy).wait_recv()
        return carry

    lax.fori_loop(0, ngy - 1, go4, 0)
    r4[j] = b4[j]

    def stage_two(c, carry):
        at = pl.multiple_of(16 + 8 * c, 8)
        here = pl.ds(at, 8)
        open_cells = ext[4, here, 0:256]
        for v, (value, rate) in enumerate(rates(mid, at, 8)):
            adv[v, here, :] = open_cells * (adv[v, here, :] - 0.25 * rate[:, 0:256])
        return carry

    lax.fori_loop(0, 16, stage_two, 0)
    ob[0] = adv[0, 16:144, :].astype(BF16)
    out_first = pltpu.make_async_copy(ob.at[0], out.at[0], o_sem.at[0])
    out_first.start()
    border_down.wait()
    border_up.wait()

    lax.fori_loop(1, ngy, got4, 0)
    for g in range(ngy):
        s4[2 * ns * g : 2 * ns * g + 2 * ns, :] = r4[g]
    sb[...] = jnp.transpose(s4[...])[0:PX]
    start2, relay2, rest2, finish2 = gather(sb, i, sg, w_send, w_recv)
    start2()
    sg[place] = sb[...]
    pacc[...] = -es[4 : 4 + PX, :]
    relay2()

    def unfold(half_at):
        lines = sg[pl.ds(half_at, chips)].reshape(chips * PX, 128)
        mixed = dot3(parts(lines), (dxs[0], dxs[1]))
        pressure = pacc[...]
        for m in range(chips):
            rows = slice(m * PX, (m + 1) * PX)
            cosine = cxs[pl.ds(half_at + m, 1), :]
            sine = cxs[pl.ds(ngx + half_at + m, 1), :]
            pressure = pressure + (mixed[rows, 0:256] * cosine - mixed[rows, 256:512] * sine)
        pacc[...] = pressure

    unfold(parity * chips)
    rest2()
    unfold(chips - parity * chips)
    wide = lax.broadcasted_iota(jnp.int32, (PX, 256), 1)
    alternate = jnp.where(wide % 2 == 0, 1.0, -1.0)
    packed_lines = sg[0]
    pressure = pacc[...] - packed_lines[:, 0:1] + packed_lines[:, ns : ns + 1] * alternate

    along = dot3(parts(pressure), (ax[0], ax[1]))
    along = jnp.concatenate([along, jnp.zeros((128 - PX, 384), F32)], axis=0)
    source = dot3((ay[0], ay[1]), parts(along))
    qs[16:152, :] = 0.5 * ext[4, 16:152, :] * source[0:136]
    qs[8:16, :] = 0.5 * ext[4, 8:16, :] * source[248:256]
    qs[0:8, :] = jnp.zeros((8, 384), F32)
    qs[152:160, :] = jnp.zeros((8, 384), F32)

    def last(c, carry):
        at = pl.multiple_of(16 + 16 * c, 16)
        here = pl.ds(at, 16)
        there = pl.ds(pl.multiple_of(16 * c, 16), 16)
        window = qs[pl.ds(pl.multiple_of(at - 8, 8), 32), :]
        half_source = window[8:24]
        quarter = 0.25 * ext[4, here, 0:256]
        change_x = quarter * slope_x(half_source)[:, 0:256]
        change_y = quarter * slope_y(window, 16)[:, 0:256]
        ob[1, there, :] = (adv[1, here, :] - change_x).astype(BF16)
        ob[2, there, :] = (adv[2, here, :] - change_y).astype(BF16)
        ob[3, there, :] = (adv[3, here, :] + half_source[:, 0:256] - 0.3 * change_x).astype(BF16)
        return carry

    outs = [out_first]
    for n in range(2):
        lax.fori_loop(4 * n, 4 * n + 4, last, 0)
        rows = pl.ds(64 * n, 64)
        outs.append(
            pltpu.make_async_copy(ob.at[pl.ds(1, 3), rows], out.at[pl.ds(1, 3), rows], o_sem.at[1 + n])
        )
        outs[-1].start()
    for copy in outs:
        copy.wait()

    finish1()
    finish2()

    def left3(k, carry):
        send3(k).wait_send()
        return carry

    def left4(k, carry):
        send4(k).wait_send()
        return carry

    lax.fori_loop(1, ngy, left3, 0)
    lax.fori_loop(1, ngy, left4, 0)


def solution(mesh):
    ngx, ngy = mesh.shape["gx"], mesh.shape["gy"]
    ns, half = 64 // ngy, ngy // 2 + 1
    rpm = 2 * ns
    consts = tables(ngx, ngy)

    def shards(velocity, weights_x, weights_y, acoustic, wall_mask):
        vel = velocity.reshape(2, 64, 128)
        ac = acoustic.reshape(4, 128, 256)
        wall = wall_mask.reshape(128, 256)
        fx, wx, sums, twf, yf, twi, yi, dx, cx = [jnp.asarray(c) for c in consts]
        anywhere = pl.BlockSpec(memory_space=pl.ANY)
        vmem = pltpu.VMEM
        dma = pltpu.SemaphoreType.DMA
        scratch = [
            vmem((ngx, 2, 64, 128), F32),
            vmem((4, 128, 256), BF16),
            vmem((128, 256), jnp.int32),
            vmem((4, 256 * ngx), F32),
            vmem((4, 128 * ngy), F32),
            vmem(fx.shape[1:], F32),
            vmem(wx.shape, BF16),
            vmem(sums.shape, BF16),
            vmem(twf.shape, F32),
            vmem(yf.shape, BF16),
            vmem(twi.shape, F32),
            vmem(yi.shape, BF16),
            vmem(dx.shape, BF16),
            vmem(cx.shape[1:], F32),
            vmem((5, 160, 384), F32),
            vmem((4, 160, 384), F32),
            vmem((4, 160, 256), F32),
            vmem((2, 144, 128), F32),
            vmem((2, 144, 128), F32),
            vmem((2, 256, 384), BF16),
            vmem((2, 256, 128), BF16),
            vmem((half, rpm, 128), F32),
            vmem((half, rpm, 128), F32),
            vmem((5, 64, 128), F32),
            vmem((ngy * rpm, 128), F32),
            vmem((ngy, rpm, 128), F32),
            vmem((ngy, rpm, 128), F32),
            vmem((half * rpm, 256), F32),
            vmem((half * 2 * ns, 256), F32),
            vmem((half * 2 * ns, 256), F32),
            vmem((ngy, 2 * ns, 128), F32),
            vmem((ngy, 2 * ns, 128), F32),
            vmem((128, 128), F32),
            vmem((PX, 128), F32),
            vmem((ngx, PX, 128), F32),
            vmem((PX, 256), F32),
            vmem((160, 384), F32),
            vmem((80, 256), F32),
            vmem((4, 128, 256), BF16),
            dma((14,)),
            dma((ngx,)), dma((ngx,)),
            dma((ngy,)), dma((ngy,)),
            dma((4,)), dma((4,)),
            dma((ngy,)), dma((ngy,)),
            dma((ngx,)), dma((ngx,)),
            dma((2,)), dma((2,)),
            dma((3,)),
            pltpu.SemaphoreType.REGULAR,
        ]
        result = pl.pallas_call(
            functools.partial(kernel, ngx, ngy),
            out_shape=jax.ShapeDtypeStruct((4, 128, 256), BF16),
            in_specs=[anywhere] * 14,
            out_specs=anywhere,
            scratch_shapes=scratch,
            compiler_params=pltpu.CompilerParams(
                collective_id=0, has_side_effects=True
            ),
            name="poisson_step",
        )(vel, weights_x, weights_y, ac, wall, fx, wx, sums, twf, yf, twi, yi, dx, cx)
        return result.reshape(4, 1, 128, 256)

    in_specs = (P(None, None, "gy", "gx"), P(), P(), P(None, None, "gy", "gx"), P(None, "gy", "gx"))
    return jax.shard_map(
        shards, mesh=mesh, in_specs=in_specs, out_specs=P(None, None, "gy", "gx"), check_vma=False
    )
```
